256 devices in a mesh: row: 16 (over z, x_hi), col: 8 (over y, core), mode: 2 (over x_lo).
Axes of the slice: x: 4 (x_hi: 2, x_lo: 2; x = x_hi * 2 + x_lo), y: 4, z: 8, core: 2. Of those that a mesh axis runs over, the one named last changes fastest.
Arguments:
- objects: float32 [2, 2, 4096, 2048], P(None, None, 'row', 'col'), may hold values from -4 to 4
- probes: float32 [2, 2, 128, 128], P('mode'), may hold values from -3 to 3
- phase: float32 [128, 128], replicated, may hold values from -3.140625 to 3.140625
- offsets: int32 [16, 8, 8, 2], P('row', 'col'), may hold values from 0 to 255
- measured: float32 [16, 8, 8, 128, 128], P('row', 'col'), may hold values from 0 to 2
Outputs:
- gradient: float32 [2, 2, 4096, 2048], P(None, None, 'row', 'col')
The draws below stay inside these ranges and needn't reach their ends.
Inputs may be any that keep to these rules, and one draw needn't show every extreme that they name: `offsets`: windows start inside their own tile of 256 x 256 cells and reach up to 127 cells into the next tiles down and to the right.
All inputs are finite; a program needn't handle non-finite values.
Results may differ from the reference program's by a relative error of at most 0.0001.
Values sent between devices are 32-bit elements; how exact they have to be, the bound alone decides.
A program may use at most 64 MiB of HBM per device.

```python
import jax
import jax.numpy as jnp
from jax import lax

TILE = 256
POS = 8
WIN = 128
SLICES = 2
MODES = 2
NR = 4096
NC = 2048
TR = 16
TC = 8
N_ROW = 16
N_COL = 8


def plant(result, own_key, least, largest):
    longest = result.shape.index(max(result.shape))
    spots = []
    for shift in (0, 1):
        where = [jax.random.randint(jax.random.fold_in(own_key, axis), (), 0, length) for axis, length in enumerate(result.shape)]
        where[longest] = (where[longest] + shift) % result.shape[longest]
        spots.append(tuple(where))
    return result.at[spots[0]].set(least).at[spots[1]].set(largest)


def block_levels(stream_key, dims, shards, least, largest):
    factor_of, own = 1.0, jax.random.fold_in(stream_key, 6)
    for axis_at, blocks in shards:
        draws = jnp.exp(jax.random.uniform(jax.random.fold_in(own, axis_at), (blocks,), jnp.float32, least / len(shards), largest / len(shards)))
        factor_of = factor_of * jnp.repeat(draws, dims[axis_at] // blocks).reshape([-1 if axis == axis_at else 1 for axis in range(len(dims))])
    return factor_of


def scatter_about(own_key, extent, scale, reach, shards=(), kind=jnp.bfloat16):
    array = jax.random.normal(own_key, extent, jnp.float32) * scale
    if len(shards) > 0:
        array = block_levels(own_key, extent, shards, -0.22, 0.18) * array
    return jnp.clip(array, min=-reach, max=reach).astype(kind)


def setup_inputs(seed: int = 0) -> dict:
    splits = jax.random.split(jax.random.key(seed), 6)
    return {
        "objects": scatter_about(splits[0], (SLICES, 2, NR, NC), 0.7, 4.0, ((2, 16), (3, 8)), jnp.float32),
        "probes": scatter_about(splits[1], (MODES, 2, WIN, WIN), 0.5, 3.0, ((0, 2),), jnp.float32),
        "phase": jnp.clip(jax.random.uniform(splits[2], (WIN, WIN), jnp.float32, -3.140625, 3.140625), -3.140625, 3.140625),
        "offsets": plant(jax.random.randint(splits[3], (TR, TC, POS, 2), 0, TILE), jax.random.fold_in(splits[3], 1), 0, TILE - 1).astype(jnp.int32),
        "measured": jnp.clip(2.0 * jax.random.uniform(splits[4], (TR, TC, POS, WIN, WIN), jnp.float32) ** block_levels(splits[4], (TR, TC, POS, WIN, WIN), ((0, 16), (1, 8)), -0.2, 0.2), 0.0, 2.0),
    }


def forward_two(field):
    return jnp.fft.fft2(field, norm="ortho")


def inverse_two(field):
    return jnp.fft.ifft2(field, norm="ortho")


def reference(objects, probes, phase, offsets, measured):
    object_c = objects[:, 0] + 1j * objects[:, 1]
    padded = jnp.pad(object_c, ((0, 0), (0, WIN), (0, WIN)))
    probe_c = probes[:, 0] + 1j * probes[:, 1]
    propagator = jnp.cos(phase) + 1j * jnp.sin(phase)
    tile_rows = (jnp.arange(N_ROW, dtype=jnp.int32) * TILE)[:, None, None]
    tile_cols = (jnp.arange(N_COL, dtype=jnp.int32) * TILE)[None, :, None]
    start_rows = (offsets[..., 0].astype(jnp.int32) + tile_rows).reshape(-1)
    start_cols = (offsets[..., 1].astype(jnp.int32) + tile_cols).reshape(-1)
    measured_flat = measured.reshape(-1, WIN, WIN)
    zero_index = jnp.int32(0)

    def advance(carry, item):
        row_start, col_start, target = item
        window = lax.dynamic_slice(padded, (zero_index, row_start, col_start), (SLICES, WIN, WIN))
        first = probe_c * window[0]
        middle = inverse_two(propagator * forward_two(first))
        exit_wave = middle * window[1]
        far_field = forward_two(exit_wave)
        intensity = jnp.sum(jnp.abs(far_field) ** 2, axis=0)
        resid = intensity - target
        grad_far = 4.0 * resid * far_field
        grad_exit = inverse_two(grad_far)
        grad_second = jnp.sum(grad_exit * jnp.conj(middle), axis=0)
        grad_middle = grad_exit * jnp.conj(window[1])
        grad_first = inverse_two(jnp.conj(propagator) * forward_two(grad_middle))
        grad_one = jnp.sum(grad_first * jnp.conj(probe_c), axis=0)
        patch = jnp.stack([grad_one, grad_second])
        current = lax.dynamic_slice(carry, (zero_index, row_start, col_start), (SLICES, WIN, WIN))
        carry = lax.dynamic_update_slice(carry, current + patch, (zero_index, row_start, col_start))
        return carry, None

    initial = jnp.zeros(padded.shape, dtype=padded.dtype)
    total, _ = lax.scan(advance, initial, (start_rows, start_cols, measured_flat))
    inside = total[:, :NR, :NC]
    return jnp.stack([jnp.real(inside), jnp.imag(inside)], axis=1).astype(objects.dtype)
```

```python
import functools
import math

import jax
import jax.numpy as jnp
import numpy as np
from jax import lax
from jax.experimental import pallas as pl
from jax.experimental.pallas import tpu as pltpu
from jax.sharding import PartitionSpec as P

WIN = 128
LANES = 128
STEP = 2


def fourier_tables():
    counter = np.arange(WIN)
    angle = 2.0 * math.pi * (np.outer(counter, counter) % WIN) / WIN
    table_re, table_im = np.cos(angle) / math.sqrt(WIN), -np.sin(angle) / math.sqrt(WIN)
    forward = np.block([[table_re, table_im], [-table_im, table_re]])

    def parts(matrix):
        high = matrix.astype(jnp.bfloat16)
        return high, (matrix - high.astype(np.float64)).astype(jnp.bfloat16)

    f_high, f_low = parts(forward)
    i_high, i_low = parts(forward.T)
    right = np.stack([np.concatenate([f_high, f_high, f_low], 0), np.concatenate([i_high, i_high, i_low], 0)])
    left = np.stack([np.concatenate([i_high, i_high, i_low], 1), np.concatenate([f_high, f_high, f_low], 1)])
    return right, left


def halves(value):
    high = value.astype(jnp.bfloat16)
    return high, (value - high.astype(jnp.float32)).astype(jnp.bfloat16)


def along_rows(value, table):
    high, low = halves(value)
    return jnp.dot(jnp.concatenate([high, low, high], 1), table, preferred_element_type=jnp.float32)


def along_columns(value, table):
    high, low = halves(value)
    return jnp.dot(table, jnp.concatenate([high, low, high], 0), preferred_element_type=jnp.float32)


def beside_form(fields):
    return jnp.concatenate([jnp.concatenate(pair, 1) for pair in fields], 0)


def stacked_form(fields):
    return jnp.concatenate([jnp.concatenate(pair, 0) for pair in fields], 1)


def from_beside(value):
    return [
        (value[at : at + WIN, :WIN], value[at : at + WIN, WIN:])
        for at in range(0, value.shape[0], WIN)
    ]


def from_stacked(value):
    return [
        (value[:WIN, at : at + WIN], value[WIN:, at : at + WIN])
        for at in range(0, value.shape[1], WIN)
    ]


def forward_two(fields, right, left):
    rows_done = from_beside(along_rows(beside_form(fields), right[0]))
    return from_stacked(along_columns(stacked_form(rows_done), left[0]))


def inverse_two(fields, right, left):
    columns_done = from_stacked(along_columns(stacked_form(fields), left[1]))
    return from_beside(along_rows(beside_form(columns_done), right[1]))


def times(a, b):
    return a[0] * b[0] - a[1] * b[1], a[0] * b[1] + a[1] * b[0]


def times_conj(a, b):
    return a[0] * b[0] + a[1] * b[1], a[1] * b[0] - a[0] * b[1]


def kernel(
    offsets, objects, probes, phase, measured, rim_right, rim_low, right, left,
    own_out, right_out, low_out,
    ext, middle, prop, spread, total, target, sems,
):
    count = measured.shape[0]
    copies = []

    def fetch(src, dst):
        copy = pltpu.make_async_copy(src, dst, sems.at[len(copies)])
        copy.start()
        copies.append(copy)

    for s in range(2):
        for j in range(2):
            fetch(objects.at[s, :, :, pl.ds(LANES * j, LANES)], ext.at[s, :, j, pl.ds(0, 256), :])
        fetch(rim_right.at[s], ext.at[s, :, 2, pl.ds(0, 256), :])
        for j in range(3):
            fetch(rim_low.at[s, :, :, pl.ds(LANES * j, LANES)], ext.at[s, :, j, pl.ds(256, WIN), :])
    fetch(measured, target)

    spread[...] = jnp.zeros_like(spread)
    prop[0] = jnp.cos(phase[...])
    prop[1] = jnp.sin(phase[...])
    for copy in copies:
        copy.wait()

    lane = lax.broadcasted_iota(jnp.int32, (WIN, LANES), 1)

    def window(s, p):
        r0, c0 = offsets[p, 0], offsets[p, 1]
        tile = c0 // LANES
        shift = c0 % LANES
        back = (LANES - shift) % LANES

        def part(c):
            first = pltpu.roll(ext[s, c, tile, pl.ds(r0, WIN), :], back, 1)
            second = pltpu.roll(ext[s, c, tile + 1, pl.ds(r0, WIN), :], back, 1)
            return jnp.where(lane < LANES - shift, first, second)

        return part(0), part(1)

    def leave(p, patch):
        shift = offsets[p, 1] % LANES
        for c in range(2):
            rolled = pltpu.roll(patch[c], shift, 1)
            spread[4 * p + 2 * c, pl.ds(256, WIN), :] = jnp.where(lane >= shift, rolled, 0.0)
            spread[4 * p + 2 * c + 1, pl.ds(256, WIN), :] = jnp.where(lane < shift, rolled, 0.0)

    def gather(s):
        for c in range(2):
            for j in range(3):
                def block(at, _, c=c, j=j):
                    row = at * WIN
                    value = jnp.zeros((WIN, LANES), jnp.float32)
                    for p in range(count):
                        r0, tile = offsets[p, 0], offsets[p, 1] // LANES
                        index = jnp.where(
                            tile == j, 4 * p + 2 * c, jnp.where(tile == j - 1, 4 * p + 2 * c + 1, 4 * count)
                        )
                        value += spread[index, pl.ds(256 - r0 + row, WIN), :]
                    total[s, c, j, pl.ds(pl.multiple_of(row, WIN), WIN), :] = value
                    return 0

                lax.fori_loop(0, 3, block, 0)

    modes = [(probes[m, 0], probes[m, 1]) for m in range(2)]
    passage = (prop[0], prop[1])

    def first_phase(step, _):
        for k in range(STEP):
            p = step * STEP + k
            view = window(0, p)
            spectrum = forward_two([times(mode, view) for mode in modes], right, left)
            field = inverse_two([times(passage, one) for one in spectrum], right, left)
            middle[p] = beside_form(field)
        return 0

    def second_phase(step, _):
        for k in range(STEP):
            p = step * STEP + k
            view = window(1, p)
            field = from_beside(middle[p])
            far = forward_two([times(one, view) for one in field], right, left)
            power = sum(one[0] * one[0] + one[1] * one[1] for one in far)
            weight = 4.0 * (power - target[p])
            gexit = inverse_two([(weight * one[0], weight * one[1]) for one in far], right, left)
            pieces = [times_conj(g, b) for g, b in zip(gexit, field)]
            leave(p, (pieces[0][0] + pieces[1][0], pieces[0][1] + pieces[1][1]))
            middle[p] = beside_form([times_conj(g, view) for g in gexit])
        return 0

    def third_phase(step, _):
        for k in range(STEP):
            p = step * STEP + k
            spectrum = forward_two(from_beside(middle[p]), right, left)
            wave = inverse_two([times_conj(one, passage) for one in spectrum], right, left)
            pieces = [times_conj(g, mode) for g, mode in zip(wave, modes)]
            leave(p, (pieces[0][0] + pieces[1][0], pieces[0][1] + pieces[1][1]))
        return 0

    lax.fori_loop(0, count // STEP, first_phase, 0)
    lax.fori_loop(0, count // STEP, second_phase, 0)
    gather(1)
    lax.fori_loop(0, count // STEP, third_phase, 0)
    gather(0)

    copies.clear()
    for s in range(2):
        for j in range(2):
            fetch(total.at[s, :, j, pl.ds(0, 256), :], own_out.at[s, :, :, pl.ds(LANES * j, LANES)])
        fetch(total.at[s, :, 2, pl.ds(0, 256), :], right_out.at[s])
        for j in range(3):
            fetch(total.at[s, :, j, pl.ds(256, WIN), :], low_out.at[s, :, :, pl.ds(LANES * j, LANES)])
    for copy in copies:
        copy.wait()


def tile_gradient(offsets, objects, probes, phase, measured, rim_right, rim_low):
    right, left = fourier_tables()
    count = measured.shape[0]
    anywhere = pl.BlockSpec(memory_space=pl.ANY)
    whole = pl.BlockSpec(memory_space=pltpu.VMEM)
    shape = jax.ShapeDtypeStruct
    return pl.pallas_call(
        kernel,
        out_shape=(
            shape((2, 2, 256, 256), jnp.float32),
            shape((2, 2, 256, WIN), jnp.float32),
            shape((2, 2, WIN, 384), jnp.float32),
        ),
        in_specs=[
            pl.BlockSpec(memory_space=pltpu.SMEM), anywhere, whole, whole, anywhere, anywhere, anywhere, whole, whole,
        ],
        out_specs=(anywhere, anywhere, anywhere),
        scratch_shapes=[
            pltpu.VMEM((2, 2, 3, 384, LANES), jnp.float32),
            pltpu.VMEM((count, 256, 256), jnp.float32),
            pltpu.VMEM((2, WIN, WIN), jnp.float32),
            pltpu.VMEM((4 * count + 1, 640, LANES), jnp.float32),
            pltpu.VMEM((2, 2, 3, 384, LANES), jnp.float32),
            pltpu.VMEM((count, WIN, WIN), jnp.float32),
            pltpu.SemaphoreType.DMA((16,)),
        ],
        compiler_params=pltpu.CompilerParams(vmem_limit_bytes=60 * 2**20),
        name="tile_gradient",
    )(offsets, objects, probes, phase, measured, rim_right, rim_low, jnp.asarray(right), jnp.asarray(left))


def on_device(objects, probes, phase, offsets, measured):
    rows, cols = lax.axis_size("row"), lax.axis_size("col")
    tile_len = objects.shape[2]
    leftward = [(i, i - 1) for i in range(1, cols)]
    rightward = [(j, i) for i, j in leftward]
    upward = [(2 * i + m, 2 * (i - 1) + 1 - m) for i in range(1, rows) for m in range(2)]
    downward = [(j, i) for i, j in upward]

    other = lax.ppermute(probes, "mode", [(0, 1), (1, 0)])
    is_first = lax.axis_index("mode") == 0
    both = jnp.concatenate([jnp.where(is_first, probes, other), jnp.where(is_first, other, probes)], 0)
    rim_right = lax.ppermute(objects[:, :, :, :WIN], "col", leftward)
    top = jnp.concatenate([objects[:, :, :WIN], rim_right[:, :, :WIN]], 3)
    rim_low = lax.ppermute(top, ("row", "mode"), upward)

    own, beside, below = tile_gradient(offsets[0, 0], objects, both, phase, measured[0, 0], rim_right, rim_low)

    fallen = lax.ppermute(below, ("row", "mode"), downward)
    beside = beside.at[:, :, :WIN].add(fallen[:, :, :, tile_len:])
    moved = lax.ppermute(beside, "col", rightward)
    own = own.at[:, :, :WIN].add(fallen[:, :, :, :tile_len])
    return own.at[:, :, :, :WIN].add(moved)


def solution(mesh):
    placed = (
        P(None, None, "row", "col"),
        P("mode", None, None, None),
        P(),
        P("row", "col", None, None),
        P("row", "col", None, None, None),
    )
    return jax.shard_map(
        on_device,
        mesh=mesh,
        in_specs=placed,
        out_specs=P(None, None, "row", "col"),
        check_vma=False,
    )
```

```python
import functools
import math

import jax
import jax.numpy as jnp
import numpy as np
from jax import lax
from jax.experimental import pallas as pl
from jax.experimental.pallas import tpu as pltpu
from jax.sharding import PartitionSpec as P

WIN = 128
LANES = 128
STEP = 2
MESH = pl.DeviceIdType.MESH


def fourier_tables():
    counter = np.arange(WIN)
    angle = 2.0 * math.pi * (np.outer(counter, counter) % WIN) / WIN
    table_re, table_im = np.cos(angle) / math.sqrt(WIN), -np.sin(angle) / math.sqrt(WIN)
    forward = np.block([[table_re, table_im], [-table_im, table_re]])

    def parts(matrix):
        high = matrix.astype(jnp.bfloat16)
        return high, (matrix - high.astype(np.float64)).astype(jnp.bfloat16)

    f_high, f_low = parts(forward)
    i_high, i_low = parts(forward.T)
    right = np.stack([np.concatenate([f_high, f_high, f_low], 0), np.concatenate([i_high, i_high, i_low], 0)])
    left = np.stack([np.concatenate([i_high, i_high, i_low], 1), np.concatenate([f_high, f_high, f_low], 1)])
    return right, left


def halves(value):
    high = value.astype(jnp.bfloat16)
    return high, (value - high.astype(jnp.float32)).astype(jnp.bfloat16)


def along_rows(value, table):
    high, low = halves(value)
    return jnp.dot(jnp.concatenate([high, low, high], 1), table, preferred_element_type=jnp.float32)


def along_columns(value, table):
    high, low = halves(value)
    return jnp.dot(table, jnp.concatenate([high, low, high], 0), preferred_element_type=jnp.float32)


def beside_form(fields):
    return jnp.concatenate([jnp.concatenate(pair, 1) for pair in fields], 0)


def stacked_form(fields):
    return jnp.concatenate([jnp.concatenate(pair, 0) for pair in fields], 1)


def from_beside(value):
    return [
        (value[at : at + WIN, :WIN], value[at : at + WIN, WIN:])
        for at in range(0, value.shape[0], WIN)
    ]


def from_stacked(value):
    return [
        (value[:WIN, at : at + WIN], value[WIN:, at : at + WIN])
        for at in range(0, value.shape[1], WIN)
    ]


def forward_two(fields, right, left):
    rows_done = from_beside(along_rows(beside_form(fields), right[0]))
    return from_stacked(along_columns(stacked_form(rows_done), left[0]))


def inverse_two(fields, right, left):
    columns_done = from_stacked(along_columns(stacked_form(fields), left[1]))
    return from_beside(along_rows(beside_form(columns_done), right[1]))


def times(a, b):
    return a[0] * b[0] - a[1] * b[1], a[0] * b[1] + a[1] * b[0]


def times_conj(a, b):
    return a[0] * b[0] + a[1] * b[1], a[1] * b[0] - a[0] * b[1]


def kernel(
    offsets, objects, probes, phase, measured, right_in, left_in,
    out,
    ext_first, ext_second, both, middle, angle, prop, spread, total, fallen, moved, target, right, left,
    sems, send, recv,
):
    rows, cols = lax.axis_size("row"), lax.axis_size("col")
    row, col, mode = lax.axis_index("row"), lax.axis_index("col"), lax.axis_index("mode")
    other = 1 - mode
    has_up, has_left, has_down, has_right = row > 0, col > 0, row < rows - 1, col < cols - 1
    count = target.shape[0]

    def device(d_row, d_col, which):
        return {"row": (row + d_row + rows) % rows, "col": (col + d_col + cols) % cols, "mode": which}

    up, down = device(-1, 0, other), device(1, 0, other)
    leftward, rightward = device(0, -1, mode), device(0, 1, mode)
    up_left, down_right = device(-1, -1, other), device(1, 1, other)
    partner = device(0, 0, other)

    def fetch(src, dst, k):
        return pltpu.make_async_copy(src, dst, sems.at[k])

    def remote(src, dst, k, to):
        return pltpu.make_async_remote_copy(
            src_ref=src, dst_ref=dst, send_sem=send.at[k], recv_sem=recv.at[k], device_id=to, device_id_type=MESH
        )

    below, beside = pl.ds(256, WIN), pl.ds(0, 256)
    ext = (ext_first, ext_second)

    own = [
        [fetch(objects.at[s, :, :, pl.ds(LANES * j, LANES)], ext[s].at[:, j, beside, :], 2 * s + j) for j in range(2)]
        for s in range(2)
    ]
    needed = [
        fetch(probes.at[0], both.at[mode], 4),
        fetch(right_in, right, 5),
        fetch(left_in, left, 6),
    ]
    get_phase = fetch(phase, angle, 7)
    get_target = fetch(measured.at[0, 0], target, 8)
    for copy in [get_phase, *own[0], *needed, *own[1], get_target]:
        copy.start()

    barrier = pltpu.get_barrier_semaphore()
    everyone = (up, down, leftward, rightward, up_left, down_right, partner)
    for one in everyone:
        pl.semaphore_signal(barrier, inc=1, device_id=one, device_id_type=MESH)
    pl.semaphore_wait(barrier, len(everyone))

    def in_low(s, j, which):
        return remote(
            objects.at[s, which, pl.ds(0, WIN), pl.ds(LANES * j, LANES)], ext[s].at[which, j, below, :], 8 * s + j, up
        )

    def in_corner(s, which):
        return remote(
            objects.at[s, which, pl.ds(0, WIN), pl.ds(0, LANES)], ext[s].at[which, 2, below, :], 8 * s + 2, up_left
        )

    def in_right(s, c):
        return remote(objects.at[s, c, :, pl.ds(0, LANES)], ext[s].at[c, 2, beside, :], 8 * s + 3 + c, leftward)

    def in_pass(s, j, which):
        return remote(ext[s].at[which, j, below, :], ext[s].at[which, j, below, :], 8 * s + 5 + j, partner)

    share = remote(probes.at[0], both.at[mode], 32, partner)

    def out_low(s, j, which):
        return remote(total.at[s, which, j, below, :], fallen.at[s, which, j], 16 + 8 * s + j, down)

    def out_corner(s, which):
        return remote(total.at[s, which, 2, below, :], fallen.at[s, which, 2], 16 + 8 * s + 2, down_right)

    def out_right(s, c):
        return remote(total.at[s, c, 2, beside, :], moved.at[s, c], 16 + 8 * s + 3 + c, rightward)

    def out_pass(s, j, which):
        return remote(fallen.at[s, which, j], fallen.at[s, which, j], 16 + 8 * s + 5 + j, partner)

    for s in range(2):
        @pl.when(has_up)
        def _(s=s):
            for j in range(2):
                in_low(s, j, other).start()

        @pl.when(has_left)
        def _(s=s):
            for c in range(2):
                in_right(s, c).start()

        @pl.when(has_up & has_left)
        def _(s=s):
            in_corner(s, other).start()

        if s == 0:
            share.start()

    @pl.when(jnp.logical_not(has_down))
    def _():
        for s in range(2):
            for c in range(2):
                for j in range(3):
                    ext[s][c, j, below, :] = jnp.zeros((WIN, LANES), jnp.float32)

    @pl.when(jnp.logical_not(has_right))
    def _():
        for s in range(2):
            for c in range(2):
                ext[s][c, 2, beside, :] = jnp.zeros((256, LANES), jnp.float32)

    @pl.when(has_down & jnp.logical_not(has_right))
    def _():
        for s in range(2):
            for c in range(2):
                ext[s][c, 2, below, :] = jnp.zeros((WIN, LANES), jnp.float32)

    spread[...] = jnp.zeros_like(spread)
    get_phase.wait()
    prop[0] = jnp.cos(angle[...])
    prop[1] = jnp.sin(angle[...])

    def hand_in(s, j):
        if j < 2:
            @pl.when(has_down)
            def _():
                in_low(s, j, mode).wait_recv()
                in_pass(s, j, mode).start()
        else:
            @pl.when(has_down & has_right)
            def _():
                in_corner(s, mode).wait_recv()
                in_pass(s, j, mode).start()

    def arrive_in(s):
        for copy in own[s]:
            copy.wait()

        @pl.when(has_right)
        def _():
            for c in range(2):
                in_right(s, c).wait_recv()

        @pl.when(has_down)
        def _():
            for j in range(2):
                in_pass(s, j, other).wait_recv()

        @pl.when(has_down & has_right)
        def _():
            in_pass(s, 2, other).wait_recv()

    def send_out(s):
        @pl.when(has_down)
        def _():
            for j in range(2):
                out_low(s, j, other).start()

        @pl.when(has_right)
        def _():
            for c in range(2):
                out_right(s, c).start()

        @pl.when(has_down & has_right)
        def _():
            out_corner(s, other).start()

    def hand_out(s, j):
        if j < 2:
            @pl.when(has_up)
            def _():
                out_low(s, j, mode).wait_recv()
                out_pass(s, j, mode).start()
        else:
            @pl.when(has_up & has_left)
            def _():
                out_corner(s, mode).wait_recv()
                out_pass(s, j, mode).start()

    def arrive_out(s):
        @pl.when(has_left)
        def _():
            for c in range(2):
                out_right(s, c).wait_recv()
                total[s, c, 0, beside, :] += moved[s, c]

        @pl.when(has_up)
        def _():
            for j in range(2):
                out_pass(s, j, other).wait_recv()
                for c in range(2):
                    total[s, c, j, pl.ds(0, WIN), :] += fallen[s, c, j]

        @pl.when(has_up & has_left)
        def _():
            out_pass(s, 2, other).wait_recv()
            for c in range(2):
                total[s, c, 0, pl.ds(0, WIN), :] += fallen[s, c, 2]

    def result(s):
        return [
            fetch(total.at[s, :, j, beside, :], out.at[s, :, :, pl.ds(LANES * j, LANES)], 9 + 2 * s + j)
            for j in range(2)
        ]

    lane = lax.broadcasted_iota(jnp.int32, (WIN, LANES), 1)

    def window(s, p):
        r0, c0 = offsets[0, 0, p, 0], offsets[0, 0, p, 1]
        tile = c0 // LANES
        shift = c0 % LANES
        back = (LANES - shift) % LANES

        def part(c):
            first = pltpu.roll(ext[s][c, tile, pl.ds(r0, WIN), :], back, 1)
            second = pltpu.roll(ext[s][c, tile + 1, pl.ds(r0, WIN), :], back, 1)
            return jnp.where(lane < LANES - shift, first, second)

        return part(0), part(1)

    def leave(p, patch):
        shift = offsets[0, 0, p, 1] % LANES
        for c in range(2):
            rolled = pltpu.roll(patch[c], shift, 1)
            spread[4 * p + 2 * c, pl.ds(256, WIN), :] = jnp.where(lane >= shift, rolled, 0.0)
            spread[4 * p + 2 * c + 1, pl.ds(256, WIN), :] = jnp.where(lane < shift, rolled, 0.0)

    def gather(s, blocks):
        for c in range(2):
            for j, at in blocks:
                value = jnp.zeros((WIN, LANES), jnp.float32)
                for p in range(count):
                    r0, tile = offsets[0, 0, p, 0], offsets[0, 0, p, 1] // LANES
                    index = jnp.where(
                        tile == j, 4 * p + 2 * c, jnp.where(tile == j - 1, 4 * p + 2 * c + 1, 4 * count)
                    )
                    value += spread[index, pl.ds(256 - r0 + WIN * at, WIN), :]
                total[s, c, j, pl.ds(WIN * at, WIN), :] = value

    rims = [(0, 2), (1, 2), (2, 2), (2, 0), (2, 1)]
    inside = [(0, 0), (0, 1), (1, 0), (1, 1)]

    for j in range(3):
        hand_in(0, j)
    for copy in needed:
        copy.wait()
    share.wait_recv()
    arrive_in(0)

    modes = [(both[m, 0], both[m, 1]) for m in range(2)]
    passage = (prop[0], prop[1])

    def first_phase(step, _):
        for j in range(3):
            @pl.when(step == j + 1)
            def _(j=j):
                hand_in(1, j)

        for k in range(STEP):
            p = step * STEP + k
            view = window(0, p)
            spectrum = forward_two([times(mode, view) for mode in modes], right, left)
            field = inverse_two([times(passage, one) for one in spectrum], right, left)
            middle[p] = beside_form(field)
        return 0

    def second_phase(step, _):
        for k in range(STEP):
            p = step * STEP + k
            view = window(1, p)
            field = from_beside(middle[p])
            far = forward_two([times(one, view) for one in field], right, left)
            power = sum(one[0] * one[0] + one[1] * one[1] for one in far)
            weight = 4.0 * (power - target[p])
            gexit = inverse_two([(weight * one[0], weight * one[1]) for one in far], right, left)
            pieces = [times_conj(g, b) for g, b in zip(gexit, field)]
            leave(p, (pieces[0][0] + pieces[1][0], pieces[0][1] + pieces[1][1]))
            middle[p] = beside_form([times_conj(g, view) for g in gexit])
        return 0

    def third_phase(step, _):
        for j in range(3):
            @pl.when(step == j + 1)
            def _(j=j):
                hand_out(1, j)

        for k in range(STEP):
            p = step * STEP + k
            spectrum = forward_two(from_beside(middle[p]), right, left)
            wave = inverse_two([times_conj(one, passage) for one in spectrum], right, left)
            pieces = [times_conj(g, mode) for g, mode in zip(wave, modes)]
            leave(p, (pieces[0][0] + pieces[1][0], pieces[0][1] + pieces[1][1]))
        return 0

    lax.fori_loop(0, count // STEP, first_phase, 0)
    arrive_in(1)
    get_target.wait()
    lax.fori_loop(0, count // STEP, second_phase, 0)
    gather(1, rims)
    send_out(1)
    gather(1, inside)
    lax.fori_loop(0, count // STEP, third_phase, 0)
    gather(0, rims)
    send_out(0)
    gather(0, inside)
    arrive_out(1)
    for copy in result(1):
        copy.start()
    for j in range(3):
        hand_out(0, j)
    arrive_out(0)
    for copy in result(0):
        copy.start()

    share.wait_send()
    for s in range(2):
        @pl.when(has_up)
        def _(s=s):
            for j in range(2):
                in_low(s, j, other).wait_send()
                out_pass(s, j, mode).wait_send()

        @pl.when(has_left)
        def _(s=s):
            for c in range(2):
                in_right(s, c).wait_send()

        @pl.when(has_up & has_left)
        def _(s=s):
            in_corner(s, other).wait_send()
            out_pass(s, 2, mode).wait_send()

        @pl.when(has_down)
        def _(s=s):
            for j in range(2):
                in_pass(s, j, mode).wait_send()
                out_low(s, j, other).wait_send()

        @pl.when(has_right)
        def _(s=s):
            for c in range(2):
                out_right(s, c).wait_send()

        @pl.when(has_down & has_right)
        def _(s=s):
            in_pass(s, 2, mode).wait_send()
            out_corner(s, other).wait_send()

        for copy in result(s):
            copy.wait()


def on_device(objects, probes, phase, offsets, measured):
    right, left = fourier_tables()
    count = measured.shape[2]
    anywhere = pl.BlockSpec(memory_space=pl.ANY)
    f32 = jnp.float32
    return pl.pallas_call(
        kernel,
        out_shape=jax.ShapeDtypeStruct(objects.shape, f32),
        in_specs=[pl.BlockSpec(memory_space=pltpu.SMEM)] + [anywhere] * 6,
        out_specs=anywhere,
        scratch_shapes=[
            pltpu.VMEM((2, 3, 384, LANES), f32),
            pltpu.VMEM((2, 3, 384, LANES), f32),
            pltpu.VMEM((2, 2, WIN, WIN), f32),
            pltpu.VMEM((count, 256, 256), f32),
            pltpu.VMEM((WIN, WIN), f32),
            pltpu.VMEM((2, WIN, WIN), f32),
            pltpu.VMEM((4 * count + 1, 640, LANES), f32),
            pltpu.VMEM((2, 2, 3, 384, LANES), f32),
            pltpu.VMEM((2, 2, 3, WIN, LANES), f32),
            pltpu.VMEM((2, 2, 256, LANES), f32),
            pltpu.VMEM((count, WIN, WIN), f32),
            pltpu.VMEM(right.shape, jnp.bfloat16),
            pltpu.VMEM(left.shape, jnp.bfloat16),
            pltpu.SemaphoreType.DMA((16,)),
            pltpu.SemaphoreType.DMA((33,)),
            pltpu.SemaphoreType.DMA((33,)),
        ],
        compiler_params=pltpu.CompilerParams(
            vmem_limit_bytes=60 * 2**20, collective_id=0, has_side_effects=True
        ),
        name="tile_gradient",
    )(offsets, objects, probes, phase, measured, jnp.asarray(right), jnp.asarray(left))


def solution(mesh):
    placed = (
        P(None, None, "row", "col"),
        P("mode", None, None, None),
        P(),
        P("row", "col", None, None),
        P("row", "col", None, None, None),
    )
    return jax.shard_map(
        on_device,
        mesh=mesh,
        in_specs=placed,
        out_specs=P(None, None, "row", "col"),
        check_vma=False,
    )
```

```python
import functools
import math

import jax
import jax.numpy as jnp
import numpy as np
from jax import lax
from jax.experimental import pallas as pl
from jax.experimental.pallas import tpu as pltpu
from jax.sharding import PartitionSpec as P

WIN = 128
LANES = 128
MESH = pl.DeviceIdType.MESH


def fourier_tables():
    counter = np.arange(WIN)
    angle = 2.0 * math.pi * (np.outer(counter, counter) % WIN) / WIN
    table_re, table_im = np.cos(angle) / math.sqrt(WIN), -np.sin(angle) / math.sqrt(WIN)
    forward = np.block([[table_re, table_im], [-table_im, table_re]])

    def parts(matrix):
        high = matrix.astype(jnp.bfloat16)
        return high, (matrix - high.astype(np.float64)).astype(jnp.bfloat16)

    f_high, f_low = parts(forward)
    i_high, i_low = parts(forward.T)
    right = np.stack([np.concatenate([f_high, f_high, f_low], 0), np.concatenate([i_high, i_high, i_low], 0)])
    left = np.stack([np.concatenate([i_high, i_high, i_low], 1), np.concatenate([f_high, f_high, f_low], 1)])
    return right, left


def halves(value):
    high = value.astype(jnp.bfloat16)
    return high, (value - high.astype(jnp.float32)).astype(jnp.bfloat16)


def along_rows(value, table):
    high, low = halves(value)
    return jnp.dot(jnp.concatenate([high, low, high], 1), table, preferred_element_type=jnp.float32)


def along_columns(value, table):
    high, low = halves(value)
    return jnp.dot(table, jnp.concatenate([high, low, high], 0), preferred_element_type=jnp.float32)


def beside_form(fields):
    return jnp.concatenate([jnp.concatenate(pair, 1) for pair in fields], 0)


def stacked_form(fields):
    return jnp.concatenate([jnp.concatenate(pair, 0) for pair in fields], 1)


def from_beside(value):
    return [
        (value[at : at + WIN, :WIN], value[at : at + WIN, WIN:])
        for at in range(0, value.shape[0], WIN)
    ]


def from_stacked(value):
    return [
        (value[:WIN, at : at + WIN], value[WIN:, at : at + WIN])
        for at in range(0, value.shape[1], WIN)
    ]


def times(a, b):
    return a[0] * b[0] - a[1] * b[1], a[0] * b[1] + a[1] * b[0]


def times_conj(a, b):
    return a[0] * b[0] + a[1] * b[1], a[1] * b[0] - a[0] * b[1]


def kernel(
    offsets, objects, probes, phase, measured, right_in, left_in,
    out,
    ext_first, ext_second, both, middle, angle, prop, spread, total, fallen, moved, target, right, left,
    sems, send, recv,
):
    rows, cols = lax.axis_size("row"), lax.axis_size("col")
    row, col, mode = lax.axis_index("row"), lax.axis_index("col"), lax.axis_index("mode")
    other = 1 - mode
    has_up, has_left, has_down, has_right = row > 0, col > 0, row < rows - 1, col < cols - 1
    count = target.shape[0]

    def device(d_row, d_col, which):
        return {"row": (row + d_row + rows) % rows, "col": (col + d_col + cols) % cols, "mode": which}

    up, down = device(-1, 0, other), device(1, 0, other)
    leftward, rightward = device(0, -1, mode), device(0, 1, mode)
    up_left, down_right = device(-1, -1, other), device(1, 1, other)
    partner = device(0, 0, other)

    def fetch(src, dst, k):
        return pltpu.make_async_copy(src, dst, sems.at[k])

    def remote(src, dst, k, to):
        return pltpu.make_async_remote_copy(
            src_ref=src, dst_ref=dst, send_sem=send.at[k], recv_sem=recv.at[k], device_id=to, device_id_type=MESH
        )

    below, beside = pl.ds(256, WIN), pl.ds(0, 256)
    ext = (ext_first, ext_second)

    own = [
        [fetch(objects.at[s, :, :, pl.ds(LANES * j, LANES)], ext[s].at[:, j, beside, :], 2 * s + j) for j in range(2)]
        for s in range(2)
    ]
    needed = [
        fetch(probes.at[0], both.at[mode], 4),
        fetch(right_in, right, 5),
        fetch(left_in, left, 6),
    ]
    get_phase = fetch(phase, angle, 7)
    get_target = fetch(measured.at[0, 0], target, 8)
    for copy in [get_phase, *own[0], *needed, *own[1], get_target]:
        copy.start()

    barrier = pltpu.get_barrier_semaphore()
    around = (up, down, leftward, rightward, up_left, down_right, partner)
    for one in around:
        pl.semaphore_signal(barrier, inc=1, device_id=one, device_id_type=MESH)
    pl.semaphore_wait(barrier, len(around))

    def in_low(s, j, which):
        return remote(
            objects.at[s, which, pl.ds(0, WIN), pl.ds(LANES * j, LANES)], ext[s].at[which, j, below, :], 8 * s + j, up
        )

    def in_corner(s, which):
        return remote(
            objects.at[s, which, pl.ds(0, WIN), pl.ds(0, LANES)], ext[s].at[which, 2, below, :], 8 * s + 2, up_left
        )

    def in_right(s, c):
        return remote(objects.at[s, c, :, pl.ds(0, LANES)], ext[s].at[c, 2, beside, :], 8 * s + 3 + c, leftward)

    def in_pass(s, j, which):
        return remote(ext[s].at[which, j, below, :], ext[s].at[which, j, below, :], 8 * s + 5 + j, partner)

    share = remote(probes.at[0], both.at[mode], 32, partner)

    def out_low(s, j, which):
        return remote(total.at[s, which, j, below, :], fallen.at[s, which, j], 16 + 8 * s + j, down)

    def out_corner(s, which):
        return remote(total.at[s, which, 2, below, :], fallen.at[s, which, 2], 16 + 8 * s + 2, down_right)

    def out_right(s, c):
        return remote(total.at[s, c, 2, beside, :], moved.at[s, c], 16 + 8 * s + 3 + c, rightward)

    def out_pass(s, j, which):
        return remote(fallen.at[s, which, j], fallen.at[s, which, j], 16 + 8 * s + 5 + j, partner)

    for s in range(2):
        @pl.when(has_up)
        def _(s=s):
            for j in range(2):
                in_low(s, j, other).start()

        @pl.when(has_left)
        def _(s=s):
            for c in range(2):
                in_right(s, c).start()

        @pl.when(has_up & has_left)
        def _(s=s):
            in_corner(s, other).start()

        if s == 0:
            share.start()

    @pl.when(jnp.logical_not(has_down))
    def _():
        for s in range(2):
            for c in range(2):
                for j in range(3):
                    ext[s][c, j, below, :] = jnp.zeros((WIN, LANES), jnp.float32)

    @pl.when(jnp.logical_not(has_right))
    def _():
        for s in range(2):
            for c in range(2):
                ext[s][c, 2, beside, :] = jnp.zeros((256, LANES), jnp.float32)

    @pl.when(has_down & jnp.logical_not(has_right))
    def _():
        for s in range(2):
            for c in range(2):
                ext[s][c, 2, below, :] = jnp.zeros((WIN, LANES), jnp.float32)

    @pl.when(jnp.logical_not(has_left))
    def _():
        moved[...] = jnp.zeros_like(moved)

    @pl.when(jnp.logical_not(has_up))
    def _():
        for s in range(2):
            for c in range(2):
                for j in range(2):
                    fallen[s, c, j] = jnp.zeros((WIN, LANES), jnp.float32)

    @pl.when(jnp.logical_not(has_up & has_left))
    def _():
        for s in range(2):
            for c in range(2):
                fallen[s, c, 2] = jnp.zeros((WIN, LANES), jnp.float32)

    spread[...] = jnp.zeros_like(spread)
    get_phase.wait()
    prop[0] = jnp.cos(angle[...])
    prop[1] = jnp.sin(angle[...])

    def hand_in(s, j):
        if j < 2:
            @pl.when(has_down)
            def _():
                in_low(s, j, mode).wait_recv()
                in_pass(s, j, mode).start()
        else:
            @pl.when(has_down & has_right)
            def _():
                in_corner(s, mode).wait_recv()
                in_pass(s, j, mode).start()

    def arrive_in(s):
        for copy in own[s]:
            copy.wait()

        @pl.when(has_right)
        def _():
            for c in range(2):
                in_right(s, c).wait_recv()

        @pl.when(has_down)
        def _():
            for j in range(2):
                in_pass(s, j, other).wait_recv()

        @pl.when(has_down & has_right)
        def _():
            in_pass(s, 2, other).wait_recv()

    def send_out(s):
        @pl.when(has_down)
        def _():
            for j in range(2):
                out_low(s, j, other).start()

        @pl.when(has_right)
        def _():
            for c in range(2):
                out_right(s, c).start()

        @pl.when(has_down & has_right)
        def _():
            out_corner(s, other).start()

    def hand_out(s, j):
        if j < 2:
            @pl.when(has_up)
            def _():
                out_low(s, j, mode).wait_recv()
                out_pass(s, j, mode).start()
        else:
            @pl.when(has_up & has_left)
            def _():
                out_corner(s, mode).wait_recv()
                out_pass(s, j, mode).start()

    def result(s):
        return [
            fetch(total.at[s, :, j, beside, :], out.at[s, :, :, pl.ds(LANES * j, LANES)], 9 + 2 * s + j)
            for j in range(2)
        ]

    def arrive_out(s):
        @pl.when(has_left)
        def _():
            for c in range(2):
                out_right(s, c).wait_recv()

        @pl.when(has_up)
        def _():
            for j in range(2):
                out_pass(s, j, other).wait_recv()

        @pl.when(has_up & has_left)
        def _():
            out_pass(s, 2, other).wait_recv()

        low = pl.ds(WIN, WIN)
        for c in range(2):
            for j in range(2):
                top = total[s, c, j, pl.ds(0, WIN), :] + fallen[s, c, j]
                if j == 0:
                    top = top + moved[s, c, pl.ds(0, WIN), :] + fallen[s, c, 2]
                    total[s, c, j, low, :] += moved[s, c, low, :]
                total[s, c, j, pl.ds(0, WIN), :] = top
        for copy in result(s):
            copy.start()

    lane = lax.broadcasted_iota(jnp.int32, (WIN, LANES), 1)

    def window(s, p):
        r0, c0 = offsets[0, 0, 0, p], offsets[0, 0, 1, p]
        tile = c0 // LANES
        shift = c0 % LANES
        back = (LANES - shift) % LANES

        def part(c):
            first = pltpu.roll(ext[s][c, tile, pl.ds(r0, WIN), :], back, 1)
            second = pltpu.roll(ext[s][c, tile + 1, pl.ds(r0, WIN), :], back, 1)
            return jnp.where(lane < LANES - shift, first, second)

        return part(0), part(1)

    def leave(p, patch):
        shift = offsets[0, 0, 1, p] % LANES
        for c in range(2):
            rolled = pltpu.roll(patch[c], shift, 1)
            spread[4 * p + 2 * c, pl.ds(256, WIN), :] = jnp.where(lane >= shift, rolled, 0.0)
            spread[4 * p + 2 * c + 1, pl.ds(256, WIN), :] = jnp.where(lane < shift, rolled, 0.0)

    def gather(s, blocks):
        for c in range(2):
            for j, at in blocks:
                value = jnp.zeros((WIN, LANES), jnp.float32)
                for p in range(count):
                    r0, tile = offsets[0, 0, 0, p], offsets[0, 0, 1, p] // LANES
                    index = jnp.where(
                        tile == j, 4 * p + 2 * c, jnp.where(tile == j - 1, 4 * p + 2 * c + 1, 4 * count)
                    )
                    value += spread[index, pl.ds(256 - r0 + WIN * at, WIN), :]
                total[s, c, j, pl.ds(WIN * at, WIN), :] = value

    rims = [(0, 2), (1, 2), (2, 2), (2, 0), (2, 1)]
    inside = [(0, 0), (0, 1), (1, 0), (1, 1)]

    for j in range(3):
        hand_in(0, j)
    for copy in needed:
        copy.wait()
    share.wait_recv()
    arrive_in(0)

    modes = [(both[m, 0], both[m, 1]) for m in range(2)]
    passage = (prop[0], prop[1])

    everyone = range(count)

    def rows_forward(fields):
        return from_beside(along_rows(beside_form(fields), right[0]))

    def rows_inverse(fields):
        return from_beside(along_rows(beside_form(fields), right[1]))

    def columns_forward(fields):
        return from_stacked(along_columns(stacked_form(fields), left[0]))

    def columns_inverse(fields):
        return from_stacked(along_columns(stacked_form(fields), left[1]))

    views = [window(0, p) for p in everyone]
    rows_done = rows_forward([times(one, view) for view in views for one in modes])
    hand_in(1, 0)
    spectrum = columns_forward(rows_done)
    hand_in(1, 1)
    columns_done = columns_inverse([times(passage, one) for one in spectrum])
    hand_in(1, 2)
    field = rows_inverse(columns_done)
    for p in everyone:
        middle[p] = beside_form(field[2 * p : 2 * p + 2])

    arrive_in(1)
    get_target.wait()

    views = [window(1, p) for p in everyone for _ in range(2)]
    field = [one for p in everyone for one in from_beside(middle[p])]
    far = columns_forward(rows_forward([times(one, view) for one, view in zip(field, views)]))
    back_far = []
    for p in everyone:
        pair = far[2 * p : 2 * p + 2]
        power = sum(one[0] * one[0] + one[1] * one[1] for one in pair)
        weight = 4.0 * (power - target[p])
        back_far += [(weight * one[0], weight * one[1]) for one in pair]
    back_exit = rows_inverse(columns_inverse(back_far))
    for p in everyone:
        pieces = [times_conj(back_exit[q], field[q]) for q in (2 * p, 2 * p + 1)]
        leave(p, (pieces[0][0] + pieces[1][0], pieces[0][1] + pieces[1][1]))
        middle[p] = beside_form([times_conj(back_exit[q], views[q]) for q in (2 * p, 2 * p + 1)])

    gather(1, rims)
    send_out(1)
    gather(1, inside)

    rows_done = rows_forward([one for p in everyone for one in from_beside(middle[p])])
    spectrum = columns_forward(rows_done)
    hand_out(1, 0)
    columns_done = columns_inverse([times_conj(one, passage) for one in spectrum])
    hand_out(1, 1)
    wave = rows_inverse(columns_done)
    hand_out(1, 2)
    for p in everyone:
        pieces = [times_conj(wave[2 * p + m], modes[m]) for m in range(2)]
        leave(p, (pieces[0][0] + pieces[1][0], pieces[0][1] + pieces[1][1]))

    gather(0, rims)
    send_out(0)
    gather(0, inside)
    arrive_out(1)
    for j in range(3):
        hand_out(0, j)
    arrive_out(0)

    share.wait_send()
    for s in range(2):
        @pl.when(has_up)
        def _(s=s):
            for j in range(2):
                in_low(s, j, other).wait_send()
                out_pass(s, j, mode).wait_send()

        @pl.when(has_left)
        def _(s=s):
            for c in range(2):
                in_right(s, c).wait_send()

        @pl.when(has_up & has_left)
        def _(s=s):
            in_corner(s, other).wait_send()
            out_pass(s, 2, mode).wait_send()

        @pl.when(has_down)
        def _(s=s):
            for j in range(2):
                in_pass(s, j, mode).wait_send()
                out_low(s, j, other).wait_send()

        @pl.when(has_right)
        def _(s=s):
            for c in range(2):
                out_right(s, c).wait_send()

        @pl.when(has_down & has_right)
        def _(s=s):
            in_pass(s, 2, mode).wait_send()
            out_corner(s, other).wait_send()

        for copy in result(s):
            copy.wait()


def on_device(objects, probes, phase, offsets, measured):
    right, left = fourier_tables()
    count = measured.shape[2]
    anywhere = pl.BlockSpec(memory_space=pl.ANY)
    f32 = jnp.float32
    return pl.pallas_call(
        kernel,
        out_shape=jax.ShapeDtypeStruct(objects.shape, f32),
        in_specs=[pl.BlockSpec(memory_space=pltpu.SMEM)] + [anywhere] * 6,
        out_specs=anywhere,
        scratch_shapes=[
            pltpu.VMEM((2, 3, 384, LANES), f32),
            pltpu.VMEM((2, 3, 384, LANES), f32),
            pltpu.VMEM((2, 2, WIN, WIN), f32),
            pltpu.VMEM((count, 256, 256), f32),
            pltpu.VMEM((WIN, WIN), f32),
            pltpu.VMEM((2, WIN, WIN), f32),
            pltpu.VMEM((4 * count + 1, 640, LANES), f32),
            pltpu.VMEM((2, 2, 3, 384, LANES), f32),
            pltpu.VMEM((2, 2, 3, WIN, LANES), f32),
            pltpu.VMEM((2, 2, 256, LANES), f32),
            pltpu.VMEM((count, WIN, WIN), f32),
            pltpu.VMEM(right.shape, jnp.bfloat16),
            pltpu.VMEM(left.shape, jnp.bfloat16),
            pltpu.SemaphoreType.DMA((13,)),
            pltpu.SemaphoreType.DMA((33,)),
            pltpu.SemaphoreType.DMA((33,)),
        ],
        compiler_params=pltpu.CompilerParams(
            vmem_limit_bytes=60 * 2**20, collective_id=0, has_side_effects=True
        ),
        name="tile_gradient",
    )(jnp.swapaxes(offsets, 2, 3), objects, probes, phase, measured, jnp.asarray(right), jnp.asarray(left))


def solution(mesh):
    placed = (
        P(None, None, "row", "col"),
        P("mode", None, None, None),
        P(),
        P("row", "col", None, None),
        P("row", "col", None, None, None),
    )
    return jax.shard_map(
        on_device,
        mesh=mesh,
        in_specs=placed,
        out_specs=P(None, None, "row", "col"),
        check_vma=False,
    )
```

```python
import functools
import math

import jax
import jax.numpy as jnp
import numpy as np
from jax import lax
from jax.experimental import pallas as pl
from jax.experimental.pallas import tpu as pltpu
from jax.sharding import PartitionSpec as P

WIN = 128
LANES = 128
MESH = pl.DeviceIdType.MESH

CHUNKS_FIRST = ((0, 0, 128), (1, 0, 64), (1, 64, 64))
CHUNKS_SECOND = ((0, 0, 128), (1, 0, 64), (1, 64, 64))


def fourier_tables():
    counter = np.arange(WIN)
    angle = 2.0 * math.pi * (np.outer(counter, counter) % WIN) / WIN
    table_re, table_im = np.cos(angle) / math.sqrt(WIN), -np.sin(angle) / math.sqrt(WIN)
    forward = np.block([[table_re, table_im], [-table_im, table_re]])

    def parts(matrix):
        high = matrix.astype(jnp.bfloat16)
        return high, (matrix - high.astype(np.float64)).astype(jnp.bfloat16)

    f_high, f_low = parts(forward)
    i_high, i_low = parts(forward.T)
    right = np.stack([np.concatenate([f_high, f_high, f_low], 0), np.concatenate([i_high, i_high, i_low], 0)])
    left = np.stack([np.concatenate([i_high, i_high, i_low], 1), np.concatenate([f_high, f_high, f_low], 1)])
    return right, left


def halves(value):
    high = value.astype(jnp.bfloat16)
    return high, (value - high.astype(jnp.float32)).astype(jnp.bfloat16)


def along_rows(value, table):
    high, low = halves(value)
    return jnp.dot(jnp.concatenate([high, low, high], 1), table, preferred_element_type=jnp.float32)


def along_columns(value, table):
    high, low = halves(value)
    return jnp.dot(table, jnp.concatenate([high, low, high], 0), preferred_element_type=jnp.float32)


def beside_form(fields):
    return jnp.concatenate([jnp.concatenate(pair, 1) for pair in fields], 0)


def stacked_form(fields):
    return jnp.concatenate([jnp.concatenate(pair, 0) for pair in fields], 1)


def from_beside(value):
    return [
        (value[at : at + WIN, :WIN], value[at : at + WIN, WIN:])
        for at in range(0, value.shape[0], WIN)
    ]


def from_stacked(value):
    return [
        (value[:WIN, at : at + WIN], value[WIN:, at : at + WIN])
        for at in range(0, value.shape[1], WIN)
    ]


def times(a, b):
    return a[0] * b[0] - a[1] * b[1], a[0] * b[1] + a[1] * b[0]


def times_conj(a, b):
    return a[0] * b[0] + a[1] * b[1], a[1] * b[0] - a[0] * b[1]


def kernel(
    offsets, objects, probes, phase, measured, right_in, left_in,
    out,
    ext_first, ext_second, both, middle, angle, prop, spread_first, spread_second, total, fallen, moved, target, right, left,
    sems, send, recv,
):
    rows, cols = lax.axis_size("row"), lax.axis_size("col")
    row, col, mode = lax.axis_index("row"), lax.axis_index("col"), lax.axis_index("mode")
    other = 1 - mode
    has_up, has_left, has_down, has_right = row > 0, col > 0, row < rows - 1, col < cols - 1
    count = target.shape[0]

    def device(d_row, d_col, which):
        return {"row": (row + d_row + rows) % rows, "col": (col + d_col + cols) % cols, "mode": which}

    up, down = device(-1, 0, other), device(1, 0, other)
    leftward, rightward = device(0, -1, mode), device(0, 1, mode)
    up_left, down_right = device(-1, -1, other), device(1, 1, other)
    partner = device(0, 0, other)

    def fetch(src, dst, k):
        return pltpu.make_async_copy(src, dst, sems.at[k])

    def remote(src, dst, k, to):
        return pltpu.make_async_remote_copy(
            src_ref=src, dst_ref=dst, send_sem=send.at[k], recv_sem=recv.at[k], device_id=to, device_id_type=MESH
        )

    below, beside = pl.ds(256, WIN), pl.ds(0, 256)
    ext = (ext_first, ext_second)
    spread = (spread_first, spread_second)
    chunks = (CHUNKS_FIRST, CHUNKS_SECOND)
    direct = tuple([j for j in range(3) if all(chunk[0] != j for chunk in part)] for part in chunks)

    own = [
        [fetch(objects.at[s, :, :, pl.ds(LANES * j, LANES)], ext[s].at[:, j, beside, :], 2 * s + j) for j in range(2)]
        for s in range(2)
    ]
    needed = [
        fetch(probes.at[0], both.at[mode], 4),
        fetch(right_in, right, 5),
        fetch(left_in, left, 6),
    ]
    get_phase = fetch(phase, angle, 7)
    get_target = fetch(measured.at[0, 0], target, 8)
    for copy in [get_phase, *own[0], *needed, *own[1], get_target]:
        copy.start()

    barrier = pltpu.get_barrier_semaphore()
    number = jnp.int32(1)
    pl.semaphore_signal(barrier, inc=1, device_id=partner, device_id_type=MESH)
    for one, there in ((down, has_down), (rightward, has_right), (down_right, has_down & has_right)):
        @pl.when(there)
        def _(one=one):
            pl.semaphore_signal(barrier, inc=1, device_id=one, device_id_type=MESH)
    for there in (has_up, has_left, has_up & has_left):
        number += there.astype(jnp.int32)
    pl.semaphore_wait(barrier, number)

    known = {}

    def linked(name, src, dst, to):
        return remote(src, dst, known.setdefault(name, len(known)), to)

    def in_low(s, chunk, which):
        j, at, size = chunk
        src = objects.at[s, which, pl.ds(at, size), pl.ds(LANES * (j % 2), LANES)]
        return linked(("in", s, chunk), src, ext[s].at[which, j, pl.ds(256 + at, size), :], up_left if j == 2 else up)

    def in_direct(s, j, c):
        src = objects.at[s, c, pl.ds(0, WIN), pl.ds(LANES * (j % 2), LANES)]
        return linked(("in direct", s, j, c), src, ext[s].at[c, j, below, :], up_left if j == 2 else up)

    def in_right(s, c):
        return linked(
            ("in right", s, c), objects.at[s, c, :, pl.ds(0, LANES)], ext[s].at[c, 2, beside, :], leftward
        )

    def in_pass(s, chunk, which):
        j, at, size = chunk
        part = ext[s].at[which, j, pl.ds(256 + at, size), :]
        return linked(("in pass", s, chunk), part, part, partner)

    share = linked("share", probes.at[0], both.at[mode], partner)

    def out_low(s, chunk, which):
        j, at, size = chunk
        src = total.at[s, which, j, pl.ds(256 + at, size), :]
        return linked(
            ("out", s, chunk), src, fallen.at[s, which, j, pl.ds(at, size), :], down_right if j == 2 else down
        )

    def out_direct(s, j, c):
        return linked(
            ("out direct", s, j, c), total.at[s, c, j, below, :], fallen.at[s, c, j], down_right if j == 2 else down
        )

    def out_right(s, c):
        return linked(("out right", s, c), total.at[s, c, 2, beside, :], moved.at[s, c], rightward)

    def out_pass(s, chunk, which):
        j, at, size = chunk
        part = fallen.at[s, which, j, pl.ds(at, size), :]
        return linked(("out pass", s, chunk), part, part, partner)

    def crossing(j, vertical, sideways):
        return vertical & sideways if j == 2 else vertical

    for s in range(2):
        for chunk in chunks[s]:
            @pl.when(crossing(chunk[0], has_up, has_left))
            def _(s=s, chunk=chunk):
                in_low(s, chunk, other).start()

        @pl.when(has_left)
        def _(s=s):
            for c in range(2):
                in_right(s, c).start()

        for j in direct[s]:
            @pl.when(crossing(j, has_up, has_left))
            def _(s=s, j=j):
                for c in range(2):
                    in_direct(s, j, c).start()

        if s == 0:
            share.start()

    @pl.when(jnp.logical_not(has_down))
    def _():
        for s in range(2):
            for c in range(2):
                for j in range(3):
                    ext[s][c, j, below, :] = jnp.zeros((WIN, LANES), jnp.float32)

    @pl.when(jnp.logical_not(has_right))
    def _():
        for s in range(2):
            for c in range(2):
                ext[s][c, 2, beside, :] = jnp.zeros((256, LANES), jnp.float32)

    @pl.when(has_down & jnp.logical_not(has_right))
    def _():
        for s in range(2):
            for c in range(2):
                ext[s][c, 2, below, :] = jnp.zeros((WIN, LANES), jnp.float32)

    @pl.when(jnp.logical_not(has_left))
    def _():
        moved[...] = jnp.zeros_like(moved)

    @pl.when(jnp.logical_not(has_up))
    def _():
        for s in range(2):
            for c in range(2):
                for j in range(2):
                    fallen[s, c, j] = jnp.zeros((WIN, LANES), jnp.float32)

    @pl.when(jnp.logical_not(has_up & has_left))
    def _():
        for s in range(2):
            for c in range(2):
                fallen[s, c, 2] = jnp.zeros((WIN, LANES), jnp.float32)

    for one in spread:
        one[...] = jnp.zeros_like(one)
    get_phase.wait()
    prop[0] = jnp.cos(angle[...])
    prop[1] = jnp.sin(angle[...])

    def hand_in(s, at):
        if at >= len(chunks[s]):
            return
        chunk = chunks[s][at]

        @pl.when(crossing(chunk[0], has_down, has_right))
        def _():
            in_low(s, chunk, mode).wait_recv()
            in_pass(s, chunk, mode).start()

    def arrive_in(s):
        for copy in own[s]:
            copy.wait()

        @pl.when(has_right)
        def _():
            for c in range(2):
                in_right(s, c).wait_recv()

        for chunk in chunks[s]:
            @pl.when(crossing(chunk[0], has_down, has_right))
            def _(chunk=chunk):
                in_pass(s, chunk, other).wait_recv()

        for j in direct[s]:
            @pl.when(crossing(j, has_down, has_right))
            def _(j=j):
                for c in range(2):
                    in_direct(s, j, c).wait_recv()

    def send_out(s):
        for chunk in chunks[s]:
            @pl.when(crossing(chunk[0], has_down, has_right))
            def _(chunk=chunk):
                out_low(s, chunk, other).start()

        @pl.when(has_right)
        def _():
            for c in range(2):
                out_right(s, c).start()

        for j in direct[s]:
            @pl.when(crossing(j, has_down, has_right))
            def _(j=j):
                for c in range(2):
                    out_direct(s, j, c).start()

    def hand_out(s, at):
        if at >= len(chunks[s]):
            return
        chunk = chunks[s][at]

        @pl.when(crossing(chunk[0], has_up, has_left))
        def _():
            out_low(s, chunk, mode).wait_recv()
            out_pass(s, chunk, mode).start()

    def result(s):
        return [
            fetch(total.at[s, :, j, beside, :], out.at[s, :, :, pl.ds(LANES * j, LANES)], 9 + 2 * s + j)
            for j in range(2)
        ]

    def arrive_out(s):
        @pl.when(has_left)
        def _():
            for c in range(2):
                out_right(s, c).wait_recv()

        for chunk in chunks[s]:
            @pl.when(crossing(chunk[0], has_up, has_left))
            def _(chunk=chunk):
                out_pass(s, chunk, other).wait_recv()

        for j in direct[s]:
            @pl.when(crossing(j, has_up, has_left))
            def _(j=j):
                for c in range(2):
                    out_direct(s, j, c).wait_recv()

        low = pl.ds(WIN, WIN)
        for c in range(2):
            for j in range(2):
                top = total[s, c, j, pl.ds(0, WIN), :] + fallen[s, c, j]
                if j == 0:
                    top = top + moved[s, c, pl.ds(0, WIN), :] + fallen[s, c, 2]
                    total[s, c, j, low, :] += moved[s, c, low, :]
                total[s, c, j, pl.ds(0, WIN), :] = top
        for copy in result(s):
            copy.start()

    lane = lax.broadcasted_iota(jnp.int32, (WIN, LANES), 1)

    def window(s, p):
        r0, c0 = offsets[0, 0, 0, p], offsets[0, 0, 1, p]
        tile = c0 // LANES
        shift = c0 % LANES
        back = (LANES - shift) % LANES

        def part(c):
            first = pltpu.roll(ext[s][c, tile, pl.ds(r0, WIN), :], back, 1)
            second = pltpu.roll(ext[s][c, tile + 1, pl.ds(r0, WIN), :], back, 1)
            return jnp.where(lane < LANES - shift, first, second)

        return part(0), part(1)

    def leave(s, p, patch):
        shift = offsets[0, 0, 1, p] % LANES
        for c in range(2):
            rolled = pltpu.roll(patch[c], shift, 1)
            spread[s][4 * p + 2 * c, pl.ds(256, WIN), :] = jnp.where(lane >= shift, rolled, 0.0)
            spread[s][4 * p + 2 * c + 1, pl.ds(256, WIN), :] = jnp.where(lane < shift, rolled, 0.0)

    def gather(s, blocks):
        for c in range(2):
            for j, at in blocks:
                value = jnp.zeros((WIN, LANES), jnp.float32)
                for p in range(count):
                    r0, tile = offsets[0, 0, 0, p], offsets[0, 0, 1, p] // LANES
                    index = jnp.where(
                        tile == j, 4 * p + 2 * c, jnp.where(tile == j - 1, 4 * p + 2 * c + 1, 4 * count)
                    )
                    value += spread[s][index, pl.ds(256 - r0 + WIN * at, WIN), :]
                total[s, c, j, pl.ds(WIN * at, WIN), :] = value

    rims = [(0, 2), (1, 2), (2, 2), (2, 0), (2, 1)]
    inside = [(0, 0), (0, 1), (1, 0), (1, 1)]

    for at in range(len(chunks[0])):
        hand_in(0, at)
    for copy in needed:
        copy.wait()
    share.wait_recv()
    arrive_in(0)

    modes = [(both[m, 0], both[m, 1]) for m in range(2)]
    passage = (prop[0], prop[1])

    everyone = range(count)

    def rows_forward(fields):
        return from_beside(along_rows(beside_form(fields), right[0]))

    def rows_inverse(fields):
        return from_beside(along_rows(beside_form(fields), right[1]))

    def columns_forward(fields):
        return from_stacked(along_columns(stacked_form(fields), left[0]))

    def columns_inverse(fields):
        return from_stacked(along_columns(stacked_form(fields), left[1]))

    views = [window(0, p) for p in everyone]
    rows_done = rows_forward([times(one, view) for view in views for one in modes])
    hand_in(1, 0)
    spectrum = columns_forward(rows_done)
    hand_in(1, 1)
    columns_done = columns_inverse([times(passage, one) for one in spectrum])
    hand_in(1, 2)
    field = rows_inverse(columns_done)
    for p in everyone:
        middle[p] = beside_form(field[2 * p : 2 * p + 2])

    arrive_in(1)
    get_target.wait()

    views = [window(1, p) for p in everyone for _ in range(2)]
    field = [one for p in everyone for one in from_beside(middle[p])]
    far = columns_forward(rows_forward([times(one, view) for one, view in zip(field, views)]))
    back_far = []
    for p in everyone:
        pair = far[2 * p : 2 * p + 2]
        power = sum(one[0] * one[0] + one[1] * one[1] for one in pair)
        weight = 4.0 * (power - target[p])
        back_far += [(weight * one[0], weight * one[1]) for one in pair]
    back_exit = rows_inverse(columns_inverse(back_far))
    for p in everyone:
        pieces = [times_conj(back_exit[q], field[q]) for q in (2 * p, 2 * p + 1)]
        leave(1, p, (pieces[0][0] + pieces[1][0], pieces[0][1] + pieces[1][1]))
        middle[p] = beside_form([times_conj(back_exit[q], views[q]) for q in (2 * p, 2 * p + 1)])

    gather(1, rims)
    send_out(1)

    rows_done = rows_forward([one for p in everyone for one in from_beside(middle[p])])
    spectrum = columns_forward(rows_done)
    hand_out(1, 0)
    columns_done = columns_inverse([times_conj(one, passage) for one in spectrum])
    hand_out(1, 1)
    wave = rows_inverse(columns_done)
    hand_out(1, 2)
    for p in everyone:
        pieces = [times_conj(wave[2 * p + m], modes[m]) for m in range(2)]
        leave(0, p, (pieces[0][0] + pieces[1][0], pieces[0][1] + pieces[1][1]))

    gather(0, rims)
    send_out(0)
    gather(1, inside)
    gather(0, inside)
    arrive_out(1)
    for at in range(len(chunks[0])):
        hand_out(0, at)
    arrive_out(0)

    share.wait_send()
    for s in range(2):
        for chunk in chunks[s]:
            @pl.when(crossing(chunk[0], has_up, has_left))
            def _(s=s, chunk=chunk):
                in_low(s, chunk, other).wait_send()
                out_pass(s, chunk, mode).wait_send()

            @pl.when(crossing(chunk[0], has_down, has_right))
            def _(s=s, chunk=chunk):
                in_pass(s, chunk, mode).wait_send()
                out_low(s, chunk, other).wait_send()

        @pl.when(has_left)
        def _(s=s):
            for c in range(2):
                in_right(s, c).wait_send()

        @pl.when(has_right)
        def _(s=s):
            for c in range(2):
                out_right(s, c).wait_send()

        for j in direct[s]:
            @pl.when(crossing(j, has_up, has_left))
            def _(s=s, j=j):
                for c in range(2):
                    in_direct(s, j, c).wait_send()

            @pl.when(crossing(j, has_down, has_right))
            def _(s=s, j=j):
                for c in range(2):
                    out_direct(s, j, c).wait_send()

        for copy in result(s):
            copy.wait()


def on_device(objects, probes, phase, offsets, measured):
    right, left = fourier_tables()
    count = measured.shape[2]
    anywhere = pl.BlockSpec(memory_space=pl.ANY)
    f32 = jnp.float32
    return pl.pallas_call(
        kernel,
        out_shape=jax.ShapeDtypeStruct(objects.shape, f32),
        in_specs=[pl.BlockSpec(memory_space=pltpu.SMEM)] + [anywhere] * 6,
        out_specs=anywhere,
        scratch_shapes=[
            pltpu.VMEM((2, 3, 384, LANES), f32),
            pltpu.VMEM((2, 3, 384, LANES), f32),
            pltpu.VMEM((2, 2, WIN, WIN), f32),
            pltpu.VMEM((count, 256, 256), f32),
            pltpu.VMEM((WIN, WIN), f32),
            pltpu.VMEM((2, WIN, WIN), f32),
            pltpu.VMEM((4 * count + 1, 640, LANES), f32),
            pltpu.VMEM((4 * count + 1, 640, LANES), f32),
            pltpu.VMEM((2, 2, 3, 384, LANES), f32),
            pltpu.VMEM((2, 2, 3, WIN, LANES), f32),
            pltpu.VMEM((2, 2, 256, LANES), f32),
            pltpu.VMEM((count, WIN, WIN), f32),
            pltpu.VMEM(right.shape, jnp.bfloat16),
            pltpu.VMEM(left.shape, jnp.bfloat16),
            pltpu.SemaphoreType.DMA((13,)),
            pltpu.SemaphoreType.DMA((64,)),
            pltpu.SemaphoreType.DMA((64,)),
        ],
        compiler_params=pltpu.CompilerParams(
            vmem_limit_bytes=60 * 2**20, collective_id=0, has_side_effects=True
        ),
        name="tile_gradient",
    )(jnp.swapaxes(offsets, 2, 3), objects, probes, phase, measured, jnp.asarray(right), jnp.asarray(left))


def solution(mesh):
    placed = (
        P(None, None, "row", "col"),
        P("mode", None, None, None),
        P(),
        P("row", "col", None, None),
        P("row", "col", None, None, None),
    )
    return jax.shard_map(
        on_device,
        mesh=mesh,
        in_specs=placed,
        out_specs=P(None, None, "row", "col"),
        check_vma=False,
    )
```

```python
import functools
import math

import jax
import jax.numpy as jnp
import numpy as np
from jax import lax
from jax.experimental import pallas as pl
from jax.experimental.pallas import tpu as pltpu
from jax.sharding import PartitionSpec as P

WIN = 128
LANES = 128
HALF = WIN // 2
MESH = pl.DeviceIdType.MESH

CHUNKS_FIRST = ((0, 0, 128), (1, 0, 64), (1, 64, 64))
CHUNKS_SECOND = ((0, 0, 128), (1, 0, 64), (1, 64, 64))


def fourier_tables():
    counter = np.arange(WIN)
    angle = 2.0 * math.pi * (np.outer(counter, counter) % WIN) / WIN
    table_re, table_im = np.cos(angle) / math.sqrt(WIN), -np.sin(angle) / math.sqrt(WIN)
    forward = np.block([[table_re, table_im], [-table_im, table_re]])

    def parts(matrix):
        high = matrix.astype(jnp.bfloat16)
        return high, (matrix - high.astype(np.float64)).astype(jnp.bfloat16)

    def for_rows(matrix):
        high, low = parts(matrix)
        return np.concatenate([high, high, low], 0)

    def for_columns(sign):
        angle = 2.0 * math.pi * (np.outer(np.arange(HALF), np.arange(HALF)) % HALF) / HALF
        table_re, table_im = np.cos(angle) / math.sqrt(WIN), -sign * np.sin(angle) / math.sqrt(WIN)
        high, low = parts(np.block([[table_re, -table_im], [table_im, table_re]]))
        return np.block([[high, high], [low, low]])

    right = np.stack([for_rows(forward), for_rows(forward.T)])
    left = np.stack([for_columns(1.0), for_columns(-1.0)])
    return right, left


def halves(value):
    high = value.astype(jnp.bfloat16)
    return high, (value - high.astype(jnp.float32)).astype(jnp.bfloat16)


def along_rows(value, table):
    high, low = halves(value)
    return jnp.dot(jnp.concatenate([high, low, high], 1), table, preferred_element_type=jnp.float32)


def along_columns(pieces, table):
    value = jnp.concatenate([jnp.concatenate(piece, 0) for piece in pieces], 1)
    both = jnp.dot(table, jnp.concatenate(halves(value), 0), preferred_element_type=jnp.float32)
    both = both[:WIN] + both[WIN:]
    return [
        (both[:HALF, at : at + WIN], both[HALF:, at : at + WIN]) for at in range(0, value.shape[1], WIN)
    ]


def beside_form(fields):
    return jnp.concatenate([jnp.concatenate(pair, 1) for pair in fields], 0)


def from_beside(value):
    return [
        (value[at : at + WIN, :WIN], value[at : at + WIN, WIN:])
        for at in range(0, value.shape[0], WIN)
    ]


def times(a, b):
    return a[0] * b[0] - a[1] * b[1], a[0] * b[1] + a[1] * b[0]


def times_conj(a, b):
    return a[0] * b[0] + a[1] * b[1], a[1] * b[0] - a[0] * b[1]


def kernel(
    offsets, objects, probes, phase, measured, right_in, left_in,
    out,
    ext_first, ext_second, both, middle, angle, prop, twist, spread_first, spread_second, total, fallen, moved, target, right, left,
    sems, send, recv,
):
    rows, cols = lax.axis_size("row"), lax.axis_size("col")
    row, col, mode = lax.axis_index("row"), lax.axis_index("col"), lax.axis_index("mode")
    other = 1 - mode
    has_up, has_left, has_down, has_right = row > 0, col > 0, row < rows - 1, col < cols - 1
    count = target.shape[0]

    def device(d_row, d_col, which):
        return {"row": (row + d_row + rows) % rows, "col": (col + d_col + cols) % cols, "mode": which}

    up, down = device(-1, 0, other), device(1, 0, other)
    leftward, rightward = device(0, -1, mode), device(0, 1, mode)
    up_left, down_right = device(-1, -1, other), device(1, 1, other)
    partner = device(0, 0, other)

    def fetch(src, dst, k):
        return pltpu.make_async_copy(src, dst, sems.at[k])

    def remote(src, dst, k, to):
        return pltpu.make_async_remote_copy(
            src_ref=src, dst_ref=dst, send_sem=send.at[k], recv_sem=recv.at[k], device_id=to, device_id_type=MESH
        )

    below, beside = pl.ds(256, WIN), pl.ds(0, 256)
    ext = (ext_first, ext_second)
    spread = (spread_first, spread_second)
    chunks = (CHUNKS_FIRST, CHUNKS_SECOND)
    direct = tuple([j for j in range(3) if all(chunk[0] != j for chunk in part)] for part in chunks)

    own = [
        [fetch(objects.at[s, :, :, pl.ds(LANES * j, LANES)], ext[s].at[:, j, beside, :], 2 * s + j) for j in range(2)]
        for s in range(2)
    ]
    needed = [
        fetch(probes.at[0], both.at[mode], 4),
        fetch(right_in, right, 5),
        fetch(left_in, left, 6),
    ]
    get_phase = fetch(phase, angle, 7)
    get_target = fetch(measured.at[0, 0], target, 8)
    for copy in [get_phase, *own[0], *needed, *own[1], get_target]:
        copy.start()

    barrier = pltpu.get_barrier_semaphore()
    number = jnp.int32(1)
    pl.semaphore_signal(barrier, inc=1, device_id=partner, device_id_type=MESH)
    for one, there in ((down, has_down), (rightward, has_right), (down_right, has_down & has_right)):
        @pl.when(there)
        def _(one=one):
            pl.semaphore_signal(barrier, inc=1, device_id=one, device_id_type=MESH)
    for there in (has_up, has_left, has_up & has_left):
        number += there.astype(jnp.int32)
    pl.semaphore_wait(barrier, number)

    known = {}

    def linked(name, src, dst, to):
        return remote(src, dst, known.setdefault(name, len(known)), to)

    def in_low(s, chunk, which):
        j, at, size = chunk
        src = objects.at[s, which, pl.ds(at, size), pl.ds(LANES * (j % 2), LANES)]
        return linked(("in", s, chunk), src, ext[s].at[which, j, pl.ds(256 + at, size), :], up_left if j == 2 else up)

    def in_direct(s, j, c):
        src = objects.at[s, c, pl.ds(0, WIN), pl.ds(LANES * (j % 2), LANES)]
        return linked(("in direct", s, j, c), src, ext[s].at[c, j, below, :], up_left if j == 2 else up)

    def in_right(s, c):
        return linked(
            ("in right", s, c), objects.at[s, c, :, pl.ds(0, LANES)], ext[s].at[c, 2, beside, :], leftward
        )

    def in_pass(s, chunk, which):
        j, at, size = chunk
        part = ext[s].at[which, j, pl.ds(256 + at, size), :]
        return linked(("in pass", s, chunk), part, part, partner)

    share = linked("share", probes.at[0], both.at[mode], partner)

    def out_low(s, chunk, which):
        j, at, size = chunk
        src = total.at[s, which, j, pl.ds(256 + at, size), :]
        return linked(
            ("out", s, chunk), src, fallen.at[s, which, j, pl.ds(at, size), :], down_right if j == 2 else down
        )

    def out_direct(s, j, c):
        return linked(
            ("out direct", s, j, c), total.at[s, c, j, below, :], fallen.at[s, c, j], down_right if j == 2 else down
        )

    def out_right(s, c):
        return linked(("out right", s, c), total.at[s, c, 2, beside, :], moved.at[s, c], rightward)

    def out_pass(s, chunk, which):
        j, at, size = chunk
        part = fallen.at[s, which, j, pl.ds(at, size), :]
        return linked(("out pass", s, chunk), part, part, partner)

    def crossing(j, vertical, sideways):
        return vertical & sideways if j == 2 else vertical

    for s in range(2):
        for chunk in chunks[s]:
            @pl.when(crossing(chunk[0], has_up, has_left))
            def _(s=s, chunk=chunk):
                in_low(s, chunk, other).start()

        @pl.when(has_left)
        def _(s=s):
            for c in range(2):
                in_right(s, c).start()

        for j in direct[s]:
            @pl.when(crossing(j, has_up, has_left))
            def _(s=s, j=j):
                for c in range(2):
                    in_direct(s, j, c).start()

        if s == 0:
            share.start()

    @pl.when(jnp.logical_not(has_down))
    def _():
        for s in range(2):
            for c in range(2):
                for j in range(3):
                    ext[s][c, j, below, :] = jnp.zeros((WIN, LANES), jnp.float32)

    @pl.when(jnp.logical_not(has_right))
    def _():
        for s in range(2):
            for c in range(2):
                ext[s][c, 2, beside, :] = jnp.zeros((256, LANES), jnp.float32)

    @pl.when(has_down & jnp.logical_not(has_right))
    def _():
        for s in range(2):
            for c in range(2):
                ext[s][c, 2, below, :] = jnp.zeros((WIN, LANES), jnp.float32)

    @pl.when(jnp.logical_not(has_left))
    def _():
        moved[...] = jnp.zeros_like(moved)

    @pl.when(jnp.logical_not(has_up))
    def _():
        for s in range(2):
            for c in range(2):
                for j in range(2):
                    fallen[s, c, j] = jnp.zeros((WIN, LANES), jnp.float32)

    @pl.when(jnp.logical_not(has_up & has_left))
    def _():
        for s in range(2):
            for c in range(2):
                fallen[s, c, 2] = jnp.zeros((WIN, LANES), jnp.float32)

    for one in spread:
        one[...] = jnp.zeros_like(one)
    get_phase.wait()
    for at in range(2):
        view = angle[pl.ds(at, HALF, stride=2), :]
        prop[0, pl.ds(HALF * at, HALF), :] = jnp.cos(view)
        prop[1, pl.ds(HALF * at, HALF), :] = jnp.sin(view)
    turned = lax.broadcasted_iota(jnp.int32, (HALF, WIN), 0).astype(jnp.float32) * (2.0 * math.pi / WIN)
    twist[0] = jnp.cos(turned)
    twist[1] = -jnp.sin(turned)

    def hand_in(s, at):
        if at >= len(chunks[s]):
            return
        chunk = chunks[s][at]

        @pl.when(crossing(chunk[0], has_down, has_right))
        def _():
            in_low(s, chunk, mode).wait_recv()
            in_pass(s, chunk, mode).start()

    def arrive_in(s):
        for copy in own[s]:
            copy.wait()

        @pl.when(has_right)
        def _():
            for c in range(2):
                in_right(s, c).wait_recv()

        for chunk in chunks[s]:
            @pl.when(crossing(chunk[0], has_down, has_right))
            def _(chunk=chunk):
                in_pass(s, chunk, other).wait_recv()

        for j in direct[s]:
            @pl.when(crossing(j, has_down, has_right))
            def _(j=j):
                for c in range(2):
                    in_direct(s, j, c).wait_recv()

    def send_out(s):
        for j in range(3):
            gather(s, [(j, 2)])
            for chunk in chunks[s]:
                if chunk[0] == j:
                    @pl.when(crossing(j, has_down, has_right))
                    def _(chunk=chunk):
                        out_low(s, chunk, other).start()

            if j in direct[s]:
                @pl.when(crossing(j, has_down, has_right))
                def _(j=j):
                    for c in range(2):
                        out_direct(s, j, c).start()

        gather(s, [(2, 0), (2, 1)])

        @pl.when(has_right)
        def _():
            for c in range(2):
                out_right(s, c).start()

    def hand_out(s, at):
        if at >= len(chunks[s]):
            return
        chunk = chunks[s][at]

        @pl.when(crossing(chunk[0], has_up, has_left))
        def _():
            out_low(s, chunk, mode).wait_recv()
            out_pass(s, chunk, mode).start()

    def result(s):
        return [
            fetch(total.at[s, :, j, beside, :], out.at[s, :, :, pl.ds(LANES * j, LANES)], 9 + 2 * s + j)
            for j in range(2)
        ]

    def arrive_out(s):
        @pl.when(has_left)
        def _():
            for c in range(2):
                out_right(s, c).wait_recv()

        for chunk in chunks[s]:
            @pl.when(crossing(chunk[0], has_up, has_left))
            def _(chunk=chunk):
                out_pass(s, chunk, other).wait_recv()

        for j in direct[s]:
            @pl.when(crossing(j, has_up, has_left))
            def _(j=j):
                for c in range(2):
                    out_direct(s, j, c).wait_recv()

        low = pl.ds(WIN, WIN)
        for c in range(2):
            for j in range(2):
                top = total[s, c, j, pl.ds(0, WIN), :] + fallen[s, c, j]
                if j == 0:
                    top = top + moved[s, c, pl.ds(0, WIN), :] + fallen[s, c, 2]
                    total[s, c, j, low, :] += moved[s, c, low, :]
                total[s, c, j, pl.ds(0, WIN), :] = top
        for copy in result(s):
            copy.start()

    lane = lax.broadcasted_iota(jnp.int32, (WIN, LANES), 1)

    def window(s, p):
        r0, c0 = offsets[0, 0, 0, p], offsets[0, 0, 1, p]
        tile = c0 // LANES
        shift = c0 % LANES
        back = (LANES - shift) % LANES

        def part(c):
            first = pltpu.roll(ext[s][c, tile, pl.ds(r0, WIN), :], back, 1)
            second = pltpu.roll(ext[s][c, tile + 1, pl.ds(r0, WIN), :], back, 1)
            return jnp.where(lane < LANES - shift, first, second)

        return part(0), part(1)

    def leave(s, p, patch):
        shift = offsets[0, 0, 1, p] % LANES
        for c in range(2):
            rolled = pltpu.roll(patch[c], shift, 1)
            spread[s][4 * p + 2 * c, pl.ds(256, WIN), :] = jnp.where(lane >= shift, rolled, 0.0)
            spread[s][4 * p + 2 * c + 1, pl.ds(256, WIN), :] = jnp.where(lane < shift, rolled, 0.0)

    def gather(s, blocks):
        for c in range(2):
            for j, at in blocks:
                value = jnp.zeros((WIN, LANES), jnp.float32)
                for p in range(count):
                    r0, tile = offsets[0, 0, 0, p], offsets[0, 0, 1, p] // LANES
                    index = jnp.where(
                        tile == j, 4 * p + 2 * c, jnp.where(tile == j - 1, 4 * p + 2 * c + 1, 4 * count)
                    )
                    value += spread[s][index, pl.ds(256 - r0 + WIN * at, WIN), :]
                total[s, c, j, pl.ds(WIN * at, WIN), :] = value

    inside = [(0, 0), (0, 1), (1, 0), (1, 1)]

    for at in range(len(chunks[0])):
        hand_in(0, at)
    for copy in needed:
        copy.wait()
    share.wait_recv()
    arrive_in(0)

    modes = [(both[m, 0], both[m, 1]) for m in range(2)]
    passage = (prop[0], prop[1])

    everyone = range(count)

    def rows_forward(fields):
        return from_beside(along_rows(beside_form(fields), right[0]))

    def rows_inverse(fields):
        return from_beside(along_rows(beside_form(fields), right[1]))

    def columns_forward(fields):
        turn = (twist[0], twist[1])
        pieces = []
        for re, im in fields:
            pieces.append((re[:HALF] + re[HALF:], im[:HALF] + im[HALF:]))
            pieces.append(times((re[:HALF] - re[HALF:], im[:HALF] - im[HALF:]), turn))
        done = along_columns(pieces, left[0])
        return [
            tuple(jnp.concatenate([even, odd], 0) for even, odd in zip(*done[at : at + 2]))
            for at in range(0, len(done), 2)
        ]

    def columns_inverse(fields):
        turn = (twist[0], twist[1])
        done = along_columns([(re[at : at + HALF], im[at : at + HALF]) for re, im in fields for at in (0, HALF)], left[1])
        out = []
        for at in range(0, len(done), 2):
            turned = times_conj(done[at + 1], turn)
            out.append(tuple(jnp.concatenate([e + o, e - o], 0) for e, o in zip(done[at], turned)))
        return out

    views = [window(0, p) for p in everyone]
    rows_done = rows_forward([times(one, view) for view in views for one in modes])
    hand_in(1, 0)
    spectrum = columns_forward(rows_done)
    hand_in(1, 1)
    columns_done = columns_inverse([times(passage, one) for one in spectrum])
    hand_in(1, 2)
    field = rows_inverse(columns_done)
    for p in everyone:
        middle[p] = beside_form(field[2 * p : 2 * p + 2])

    arrive_in(1)
    get_target.wait()

    views = [window(1, p) for p in everyone for _ in range(2)]
    field = [one for p in everyone for one in from_beside(middle[p])]
    far = columns_forward(rows_forward([times(one, view) for one, view in zip(field, views)]))
    back_far = []
    for p in everyone:
        pair = far[2 * p : 2 * p + 2]
        power = sum(one[0] * one[0] + one[1] * one[1] for one in pair)
        wanted = jnp.concatenate([target[p, pl.ds(at, HALF, stride=2), :] for at in range(2)], 0)
        weight = 4.0 * (power - wanted)
        back_far += [(weight * one[0], weight * one[1]) for one in pair]
    back_exit = rows_inverse(columns_inverse(back_far))
    for p in everyone:
        pieces = [times_conj(back_exit[q], field[q]) for q in (2 * p, 2 * p + 1)]
        leave(1, p, (pieces[0][0] + pieces[1][0], pieces[0][1] + pieces[1][1]))
        middle[p] = beside_form([times_conj(back_exit[q], views[q]) for q in (2 * p, 2 * p + 1)])

    send_out(1)

    rows_done = rows_forward([one for p in everyone for one in from_beside(middle[p])])
    spectrum = columns_forward(rows_done)
    hand_out(1, 0)
    columns_done = columns_inverse([times_conj(one, passage) for one in spectrum])
    hand_out(1, 1)
    wave = rows_inverse(columns_done)
    hand_out(1, 2)
    for p in everyone:
        pieces = [times_conj(wave[2 * p + m], modes[m]) for m in range(2)]
        leave(0, p, (pieces[0][0] + pieces[1][0], pieces[0][1] + pieces[1][1]))

    send_out(0)
    gather(1, inside)
    gather(0, inside)
    arrive_out(1)
    for at in range(len(chunks[0])):
        hand_out(0, at)
    arrive_out(0)

    share.wait_send()
    for s in range(2):
        for chunk in chunks[s]:
            @pl.when(crossing(chunk[0], has_up, has_left))
            def _(s=s, chunk=chunk):
                in_low(s, chunk, other).wait_send()
                out_pass(s, chunk, mode).wait_send()

            @pl.when(crossing(chunk[0], has_down, has_right))
            def _(s=s, chunk=chunk):
                in_pass(s, chunk, mode).wait_send()
                out_low(s, chunk, other).wait_send()

        @pl.when(has_left)
        def _(s=s):
            for c in range(2):
                in_right(s, c).wait_send()

        @pl.when(has_right)
        def _(s=s):
            for c in range(2):
                out_right(s, c).wait_send()

        for j in direct[s]:
            @pl.when(crossing(j, has_up, has_left))
            def _(s=s, j=j):
                for c in range(2):
                    in_direct(s, j, c).wait_send()

            @pl.when(crossing(j, has_down, has_right))
            def _(s=s, j=j):
                for c in range(2):
                    out_direct(s, j, c).wait_send()

        for copy in result(s):
            copy.wait()


def on_device(objects, probes, phase, offsets, measured):
    right, left = fourier_tables()
    count = measured.shape[2]
    anywhere = pl.BlockSpec(memory_space=pl.ANY)
    f32 = jnp.float32
    return pl.pallas_call(
        kernel,
        out_shape=jax.ShapeDtypeStruct(objects.shape, f32),
        in_specs=[pl.BlockSpec(memory_space=pltpu.SMEM)] + [anywhere] * 6,
        out_specs=anywhere,
        scratch_shapes=[
            pltpu.VMEM((2, 3, 384, LANES), f32),
            pltpu.VMEM((2, 3, 384, LANES), f32),
            pltpu.VMEM((2, 2, WIN, WIN), f32),
            pltpu.VMEM((count, 256, 256), f32),
            pltpu.VMEM((WIN, WIN), f32),
            pltpu.VMEM((2, WIN, WIN), f32),
            pltpu.VMEM((2, HALF, WIN), f32),
            pltpu.VMEM((4 * count + 1, 640, LANES), f32),
            pltpu.VMEM((4 * count + 1, 640, LANES), f32),
            pltpu.VMEM((2, 2, 3, 384, LANES), f32),
            pltpu.VMEM((2, 2, 3, WIN, LANES), f32),
            pltpu.VMEM((2, 2, 256, LANES), f32),
            pltpu.VMEM((count, WIN, WIN), f32),
            pltpu.VMEM(right.shape, jnp.bfloat16),
            pltpu.VMEM(left.shape, jnp.bfloat16),
            pltpu.SemaphoreType.DMA((13,)),
            pltpu.SemaphoreType.DMA((64,)),
            pltpu.SemaphoreType.DMA((64,)),
        ],
        compiler_params=pltpu.CompilerParams(
            vmem_limit_bytes=60 * 2**20, collective_id=0, has_side_effects=True
        ),
        name="tile_gradient",
    )(jnp.swapaxes(offsets, 2, 3), objects, probes, phase, measured, jnp.asarray(right), jnp.asarray(left))


def solution(mesh):
    placed = (
        P(None, None, "row", "col"),
        P("mode", None, None, None),
        P(),
        P("row", "col", None, None),
        P("row", "col", None, None, None),
    )
    return jax.shard_map(
        on_device,
        mesh=mesh,
        in_specs=placed,
        out_specs=P(None, None, "row", "col"),
        check_vma=False,
    )
```

```python
import functools
import math

import jax
import jax.numpy as jnp
import numpy as np
from jax import lax
from jax.experimental import pallas as pl
from jax.experimental.pallas import tpu as pltpu
from jax.sharding import PartitionSpec as P

WIN = 128
LANES = 128
HALF = WIN // 2
MESH = pl.DeviceIdType.MESH

CHUNKS_FIRST = ((0, 0, 128), (1, 0, 64), (1, 64, 64))
CHUNKS_SECOND = ((0, 0, 128), (1, 0, 64), (1, 64, 64))


def fourier_tables():
    counter = np.arange(WIN)
    angle = 2.0 * math.pi * (np.outer(counter, counter) % WIN) / WIN
    table_re, table_im = np.cos(angle) / math.sqrt(WIN), -np.sin(angle) / math.sqrt(WIN)
    forward = np.block([[table_re, table_im], [-table_im, table_re]])

    def parts(matrix):
        high = matrix.astype(jnp.bfloat16)
        return high, (matrix - high.astype(np.float64)).astype(jnp.bfloat16)

    def for_rows(matrix):
        high, low = parts(matrix)
        return np.concatenate([high, high, low], 0)

    def for_columns(sign):
        angle = 2.0 * math.pi * (np.outer(np.arange(HALF), np.arange(HALF)) % HALF) / HALF
        table_re, table_im = np.cos(angle) / math.sqrt(WIN), -sign * np.sin(angle) / math.sqrt(WIN)
        high, low = parts(np.block([[table_re, -table_im], [table_im, table_re]]))
        return np.block([[high, high], [low, low]])

    right = np.stack([for_rows(forward), for_rows(forward.T)])
    left = np.stack([for_columns(1.0), for_columns(-1.0)])
    return right, left


def halves(value):
    high = value.astype(jnp.bfloat16)
    return high, (value - high.astype(jnp.float32)).astype(jnp.bfloat16)


def along_rows(value, table):
    high, low = halves(value)
    return jnp.dot(jnp.concatenate([high, low, high], 1), table, preferred_element_type=jnp.float32)


def along_columns(pieces, table):
    value = jnp.concatenate([jnp.concatenate(piece, 0) for piece in pieces], 1)
    both = jnp.dot(table, jnp.concatenate(halves(value), 0), preferred_element_type=jnp.float32)
    both = both[:WIN] + both[WIN:]
    return [
        (both[:HALF, at : at + WIN], both[HALF:, at : at + WIN]) for at in range(0, value.shape[1], WIN)
    ]


def beside_form(fields):
    return jnp.concatenate([jnp.concatenate(pair, 1) for pair in fields], 0)


def from_beside(value):
    return [
        (value[at : at + WIN, :WIN], value[at : at + WIN, WIN:])
        for at in range(0, value.shape[0], WIN)
    ]


def times(a, b):
    return a[0] * b[0] - a[1] * b[1], a[0] * b[1] + a[1] * b[0]


def times_conj(a, b):
    return a[0] * b[0] + a[1] * b[1], a[1] * b[0] - a[0] * b[1]


def kernel(
    offsets, objects, probes, phase, measured, right_in, left_in,
    out,
    ext_first, ext_second, both, middle, angle, prop, twist, spread_first, spread_second, total, fallen, moved, target, right, left,
    sems, send, recv,
):
    rows, cols = lax.axis_size("row"), lax.axis_size("col")
    row, col, mode = lax.axis_index("row"), lax.axis_index("col"), lax.axis_index("mode")
    other = 1 - mode
    has_up, has_left, has_down, has_right = row > 0, col > 0, row < rows - 1, col < cols - 1
    count = target.shape[0]

    def device(d_row, d_col, which):
        return {"row": (row + d_row + rows) % rows, "col": (col + d_col + cols) % cols, "mode": which}

    up, down = device(-1, 0, other), device(1, 0, other)
    leftward, rightward = device(0, -1, mode), device(0, 1, mode)
    up_left, down_right = device(-1, -1, other), device(1, 1, other)
    partner = device(0, 0, other)

    def fetch(src, dst, k):
        return pltpu.make_async_copy(src, dst, sems.at[k])

    def remote(src, dst, k, to):
        return pltpu.make_async_remote_copy(
            src_ref=src, dst_ref=dst, send_sem=send.at[k], recv_sem=recv.at[k], device_id=to, device_id_type=MESH
        )

    below, beside = pl.ds(256, WIN), pl.ds(0, 256)
    ext = (ext_first, ext_second)
    spread = (spread_first, spread_second)
    chunks = (CHUNKS_FIRST, CHUNKS_SECOND)
    direct = tuple([j for j in range(3) if all(chunk[0] != j for chunk in part)] for part in chunks)

    own = [
        [fetch(objects.at[s, :, :, pl.ds(LANES * j, LANES)], ext[s].at[:, j, beside, :], 2 * s + j) for j in range(2)]
        for s in range(2)
    ]
    needed = [
        fetch(probes.at[0], both.at[mode], 4),
        fetch(right_in, right, 5),
        fetch(left_in, left, 6),
    ]
    get_phase = fetch(phase, angle, 7)
    get_target = fetch(measured.at[0, 0], target, 8)
    for copy in [get_phase, *own[0], *needed, *own[1], get_target]:
        copy.start()

    barrier = pltpu.get_barrier_semaphore()
    number = jnp.int32(1)
    pl.semaphore_signal(barrier, inc=1, device_id=partner, device_id_type=MESH)
    for one, there in ((down, has_down), (rightward, has_right), (down_right, has_down & has_right)):
        @pl.when(there)
        def _(one=one):
            pl.semaphore_signal(barrier, inc=1, device_id=one, device_id_type=MESH)
    for there in (has_up, has_left, has_up & has_left):
        number += there.astype(jnp.int32)
    pl.semaphore_wait(barrier, number)

    known = {}

    def linked(name, src, dst, to):
        return remote(src, dst, known.setdefault(name, len(known)), to)

    def in_low(s, chunk, which):
        j, at, size = chunk
        src = objects.at[s, which, pl.ds(at, size), pl.ds(LANES * (j % 2), LANES)]
        return linked(("in", s, chunk), src, ext[s].at[which, j, pl.ds(256 + at, size), :], up_left if j == 2 else up)

    def in_direct(s, j, c):
        src = objects.at[s, c, pl.ds(0, WIN), pl.ds(LANES * (j % 2), LANES)]
        return linked(("in direct", s, j, c), src, ext[s].at[c, j, below, :], up_left if j == 2 else up)

    def in_right(s, c):
        return linked(
            ("in right", s, c), objects.at[s, c, :, pl.ds(0, LANES)], ext[s].at[c, 2, beside, :], leftward
        )

    def in_pass(s, chunk, which):
        j, at, size = chunk
        part = ext[s].at[which, j, pl.ds(256 + at, size), :]
        return linked(("in pass", s, chunk), part, part, partner)

    share = linked("share", probes.at[0], both.at[mode], partner)

    def out_low(s, chunk, which):
        j, at, size = chunk
        src = total.at[s, which, j, pl.ds(256 + at, size), :]
        return linked(
            ("out", s, chunk), src, fallen.at[s, which, j, pl.ds(at, size), :], down_right if j == 2 else down
        )

    def out_direct(s, j, c):
        return linked(
            ("out direct", s, j, c), total.at[s, c, j, below, :], fallen.at[s, c, j], down_right if j == 2 else down
        )

    def out_right(s, c):
        return linked(("out right", s, c), total.at[s, c, 2, beside, :], moved.at[s, c], rightward)

    def out_pass(s, chunk, which):
        j, at, size = chunk
        part = fallen.at[s, which, j, pl.ds(at, size), :]
        return linked(("out pass", s, chunk), part, part, partner)

    def crossing(j, vertical, sideways):
        return vertical & sideways if j == 2 else vertical

    for s in range(2):
        for chunk in chunks[s]:
            @pl.when(crossing(chunk[0], has_up, has_left))
            def _(s=s, chunk=chunk):
                in_low(s, chunk, other).start()

        @pl.when(has_left)
        def _(s=s):
            for c in range(2):
                in_right(s, c).start()

        for j in direct[s]:
            @pl.when(crossing(j, has_up, has_left))
            def _(s=s, j=j):
                for c in range(2):
                    in_direct(s, j, c).start()

        if s == 0:
            share.start()

    @pl.when(jnp.logical_not(has_down))
    def _():
        for s in range(2):
            for c in range(2):
                for j in range(3):
                    ext[s][c, j, below, :] = jnp.zeros((WIN, LANES), jnp.float32)

    @pl.when(jnp.logical_not(has_right))
    def _():
        for s in range(2):
            for c in range(2):
                ext[s][c, 2, beside, :] = jnp.zeros((256, LANES), jnp.float32)

    @pl.when(has_down & jnp.logical_not(has_right))
    def _():
        for s in range(2):
            for c in range(2):
                ext[s][c, 2, below, :] = jnp.zeros((WIN, LANES), jnp.float32)

    @pl.when(jnp.logical_not(has_left))
    def _():
        moved[...] = jnp.zeros_like(moved)

    @pl.when(jnp.logical_not(has_up))
    def _():
        for s in range(2):
            for c in range(2):
                for j in range(2):
                    fallen[s, c, j] = jnp.zeros((WIN, LANES), jnp.float32)

    @pl.when(jnp.logical_not(has_up & has_left))
    def _():
        for s in range(2):
            for c in range(2):
                fallen[s, c, 2] = jnp.zeros((WIN, LANES), jnp.float32)

    for one in spread:
        one[...] = jnp.zeros_like(one)
    get_phase.wait()
    for at in range(2):
        view = angle[pl.ds(at, HALF, stride=2), :]
        prop[0, pl.ds(HALF * at, HALF), :] = jnp.cos(view)
        prop[1, pl.ds(HALF * at, HALF), :] = jnp.sin(view)
    turned = lax.broadcasted_iota(jnp.int32, (HALF, WIN), 0).astype(jnp.float32) * (2.0 * math.pi / WIN)
    twist[0] = jnp.cos(turned)
    twist[1] = -jnp.sin(turned)

    def hand_in(s, at):
        if at >= len(chunks[s]):
            return
        chunk = chunks[s][at]

        @pl.when(crossing(chunk[0], has_down, has_right))
        def _():
            in_low(s, chunk, mode).wait_recv()
            in_pass(s, chunk, mode).start()

    def arrive_in(s):
        for copy in own[s]:
            copy.wait()

        @pl.when(has_right)
        def _():
            for c in range(2):
                in_right(s, c).wait_recv()

        for chunk in chunks[s]:
            @pl.when(crossing(chunk[0], has_down, has_right))
            def _(chunk=chunk):
                in_pass(s, chunk, other).wait_recv()

        for j in direct[s]:
            @pl.when(crossing(j, has_down, has_right))
            def _(j=j):
                for c in range(2):
                    in_direct(s, j, c).wait_recv()

    def send_out(s):
        for j in range(3):
            gather(s, [(j, 2)])
            for chunk in chunks[s]:
                if chunk[0] == j:
                    @pl.when(crossing(j, has_down, has_right))
                    def _(chunk=chunk):
                        out_low(s, chunk, other).start()

            if j in direct[s]:
                @pl.when(crossing(j, has_down, has_right))
                def _(j=j):
                    for c in range(2):
                        out_direct(s, j, c).start()

        gather(s, [(2, 0), (2, 1)])

        @pl.when(has_right)
        def _():
            for c in range(2):
                out_right(s, c).start()

    def hand_out(s, at):
        if at >= len(chunks[s]):
            return
        chunk = chunks[s][at]

        @pl.when(crossing(chunk[0], has_up, has_left))
        def _():
            out_low(s, chunk, mode).wait_recv()
            out_pass(s, chunk, mode).start()

    def result(s):
        return [
            fetch(total.at[s, :, j, beside, :], out.at[s, :, :, pl.ds(LANES * j, LANES)], 9 + 2 * s + j)
            for j in range(2)
        ]

    def arrive_out(s):
        @pl.when(has_left)
        def _():
            for c in range(2):
                out_right(s, c).wait_recv()

        for chunk in chunks[s]:
            @pl.when(crossing(chunk[0], has_up, has_left))
            def _(chunk=chunk):
                out_pass(s, chunk, other).wait_recv()

        for j in direct[s]:
            @pl.when(crossing(j, has_up, has_left))
            def _(j=j):
                for c in range(2):
                    out_direct(s, j, c).wait_recv()

        low = pl.ds(WIN, WIN)
        for c in range(2):
            for j in range(2):
                top = total[s, c, j, pl.ds(0, WIN), :] + fallen[s, c, j]
                if j == 0:
                    top = top + moved[s, c, pl.ds(0, WIN), :] + fallen[s, c, 2]
                    total[s, c, j, low, :] += moved[s, c, low, :]
                total[s, c, j, pl.ds(0, WIN), :] = top
        for copy in result(s):
            copy.start()

    lane = lax.broadcasted_iota(jnp.int32, (WIN, LANES), 1)

    def window(s, p):
        r0, c0 = offsets[0, 0, 0, p], offsets[0, 0, 1, p]
        tile = c0 // LANES
        shift = c0 % LANES
        back = (LANES - shift) % LANES

        def part(c):
            first = pltpu.roll(ext[s][c, tile, pl.ds(r0, WIN), :], back, 1)
            second = pltpu.roll(ext[s][c, tile + 1, pl.ds(r0, WIN), :], back, 1)
            return jnp.where(lane < LANES - shift, first, second)

        return part(0), part(1)

    def leave(s, p, patch):
        shift = offsets[0, 0, 1, p] % LANES
        for c in range(2):
            rolled = pltpu.roll(patch[c], shift, 1)
            spread[s][4 * p + 2 * c, pl.ds(256, WIN), :] = jnp.where(lane >= shift, rolled, 0.0)
            spread[s][4 * p + 2 * c + 1, pl.ds(256, WIN), :] = jnp.where(lane < shift, rolled, 0.0)

    def gather(s, blocks):
        for c in range(2):
            for j, at in blocks:
                value = jnp.zeros((WIN, LANES), jnp.float32)
                for p in range(count):
                    r0, tile = offsets[0, 0, 0, p], offsets[0, 0, 1, p] // LANES
                    index = jnp.where(
                        tile == j, 4 * p + 2 * c, jnp.where(tile == j - 1, 4 * p + 2 * c + 1, 4 * count)
                    )
                    value += spread[s][index, pl.ds(256 - r0 + WIN * at, WIN), :]
                total[s, c, j, pl.ds(WIN * at, WIN), :] = value

    inside = [(0, 0), (0, 1), (1, 0), (1, 1)]

    for at in range(len(chunks[0])):
        hand_in(0, at)
    for copy in needed:
        copy.wait()
    share.wait_recv()
    arrive_in(0)

    modes = [(both[m, 0], both[m, 1]) for m in range(2)]
    passage = (prop[0], prop[1])

    everyone = range(count)

    def rows_forward(fields):
        return from_beside(along_rows(beside_form(fields), right[0]))

    def rows_inverse(fields):
        return from_beside(along_rows(beside_form(fields), right[1]))

    def columns_forward(fields):
        turn = (twist[0], twist[1])
        pieces = []
        for re, im in fields:
            pieces.append((re[:HALF] + re[HALF:], im[:HALF] + im[HALF:]))
            pieces.append(times((re[:HALF] - re[HALF:], im[:HALF] - im[HALF:]), turn))
        done = along_columns(pieces, left[0])
        return [
            tuple(jnp.concatenate([even, odd], 0) for even, odd in zip(*done[at : at + 2]))
            for at in range(0, len(done), 2)
        ]

    def columns_inverse(fields):
        turn = (twist[0], twist[1])
        done = along_columns([(re[at : at + HALF], im[at : at + HALF]) for re, im in fields for at in (0, HALF)], left[1])
        out = []
        for at in range(0, len(done), 2):
            turned = times_conj(done[at + 1], turn)
            out.append(tuple(jnp.concatenate([e + o, e - o], 0) for e, o in zip(done[at], turned)))
        return out

    views = [window(0, p) for p in everyone]
    waves = [times(one, view) for view in views for one in modes]
    hand_in(1, 0)
    rows_done = rows_forward(waves)
    hand_in(1, 1)
    spectrum = columns_forward(rows_done)
    hand_in(1, 2)
    columns_done = columns_inverse([times(passage, one) for one in spectrum])
    field = rows_inverse(columns_done)
    for p in everyone:
        middle[p] = beside_form(field[2 * p : 2 * p + 2])

    arrive_in(1)
    get_target.wait()

    views = [window(1, p) for p in everyone for _ in range(2)]
    field = [one for p in everyone for one in from_beside(middle[p])]
    far = columns_forward(rows_forward([times(one, view) for one, view in zip(field, views)]))
    back_far = []
    for p in everyone:
        pair = far[2 * p : 2 * p + 2]
        power = sum(one[0] * one[0] + one[1] * one[1] for one in pair)
        wanted = jnp.concatenate([target[p, pl.ds(at, HALF, stride=2), :] for at in range(2)], 0)
        weight = 4.0 * (power - wanted)
        back_far += [(weight * one[0], weight * one[1]) for one in pair]
    back_exit = rows_inverse(columns_inverse(back_far))
    for p in everyone:
        pieces = [times_conj(back_exit[q], field[q]) for q in (2 * p, 2 * p + 1)]
        leave(1, p, (pieces[0][0] + pieces[1][0], pieces[0][1] + pieces[1][1]))
        middle[p] = beside_form([times_conj(back_exit[q], views[q]) for q in (2 * p, 2 * p + 1)])

    send_out(1)

    rows_done = rows_forward([one for p in everyone for one in from_beside(middle[p])])
    spectrum = columns_forward(rows_done)
    columns_done = columns_inverse([times_conj(one, passage) for one in spectrum])
    wave = rows_inverse(columns_done)
    for p in everyone:
        pieces = [times_conj(wave[2 * p + m], modes[m]) for m in range(2)]
        leave(0, p, (pieces[0][0] + pieces[1][0], pieces[0][1] + pieces[1][1]))

    send_out(0)
    for at in range(len(chunks[1])):
        hand_out(1, at)
    gather(1, inside)
    gather(0, inside)
    arrive_out(1)
    for at in range(len(chunks[0])):
        hand_out(0, at)
    arrive_out(0)

    share.wait_send()
    for s in range(2):
        for chunk in chunks[s]:
            @pl.when(crossing(chunk[0], has_up, has_left))
            def _(s=s, chunk=chunk):
                in_low(s, chunk, other).wait_send()
                out_pass(s, chunk, mode).wait_send()

            @pl.when(crossing(chunk[0], has_down, has_right))
            def _(s=s, chunk=chunk):
                in_pass(s, chunk, mode).wait_send()
                out_low(s, chunk, other).wait_send()

        @pl.when(has_left)
        def _(s=s):
            for c in range(2):
                in_right(s, c).wait_send()

        @pl.when(has_right)
        def _(s=s):
            for c in range(2):
                out_right(s, c).wait_send()

        for j in direct[s]:
            @pl.when(crossing(j, has_up, has_left))
            def _(s=s, j=j):
                for c in range(2):
                    in_direct(s, j, c).wait_send()

            @pl.when(crossing(j, has_down, has_right))
            def _(s=s, j=j):
                for c in range(2):
                    out_direct(s, j, c).wait_send()

        for copy in result(s):
            copy.wait()


def settle(src, out, held, sems):
    parts = [(s, c) for s in range(2) for c in range(2)]
    into = [pltpu.make_async_copy(src.at[part], held.at[part], sems.at[k]) for k, part in enumerate(parts)]
    away = [pltpu.make_async_copy(held.at[part], out.at[part], sems.at[4 + k]) for k, part in enumerate(parts)]
    for copy in into:
        copy.start()
    for one, copy in zip(into, away):
        one.wait()
        copy.start()
    for copy in away:
        copy.wait()


def on_device(objects, probes, phase, offsets, measured):
    right, left = fourier_tables()
    count = measured.shape[2]
    anywhere = pl.BlockSpec(memory_space=pl.ANY)
    f32 = jnp.float32
    gradient = pl.pallas_call(
        kernel,
        out_shape=jax.ShapeDtypeStruct(objects.shape, f32),
        in_specs=[pl.BlockSpec(memory_space=pltpu.SMEM)] + [anywhere] * 6,
        out_specs=anywhere,
        scratch_shapes=[
            pltpu.VMEM((2, 3, 384, LANES), f32),
            pltpu.VMEM((2, 3, 384, LANES), f32),
            pltpu.VMEM((2, 2, WIN, WIN), f32),
            pltpu.VMEM((count, 256, 256), f32),
            pltpu.VMEM((WIN, WIN), f32),
            pltpu.VMEM((2, WIN, WIN), f32),
            pltpu.VMEM((2, HALF, WIN), f32),
            pltpu.VMEM((4 * count + 1, 640, LANES), f32),
            pltpu.VMEM((4 * count + 1, 640, LANES), f32),
            pltpu.VMEM((2, 2, 3, 384, LANES), f32),
            pltpu.VMEM((2, 2, 3, WIN, LANES), f32),
            pltpu.VMEM((2, 2, 256, LANES), f32),
            pltpu.VMEM((count, WIN, WIN), f32),
            pltpu.VMEM(right.shape, jnp.bfloat16),
            pltpu.VMEM(left.shape, jnp.bfloat16),
            pltpu.SemaphoreType.DMA((13,)),
            pltpu.SemaphoreType.DMA((64,)),
            pltpu.SemaphoreType.DMA((64,)),
        ],
        compiler_params=pltpu.CompilerParams(
            vmem_limit_bytes=60 * 2**20, collective_id=0, has_side_effects=True
        ),
        name="tile_gradient",
    )(jnp.swapaxes(offsets, 2, 3), objects, probes, phase, measured, jnp.asarray(right), jnp.asarray(left))
    return pl.pallas_call(
        settle,
        out_shape=jax.ShapeDtypeStruct(objects.shape, f32),
        in_specs=[anywhere],
        out_specs=anywhere,
        scratch_shapes=[pltpu.VMEM(objects.shape, f32), pltpu.SemaphoreType.DMA((8,))],
        compiler_params=pltpu.CompilerParams(vmem_limit_bytes=60 * 2**20),
        name="settle",
    )(gradient)


def solution(mesh):
    placed = (
        P(None, None, "row", "col"),
        P("mode", None, None, None),
        P(),
        P("row", "col", None, None),
        P("row", "col", None, None, None),
    )
    return jax.shard_map(
        on_device,
        mesh=mesh,
        in_specs=placed,
        out_specs=P(None, None, "row", "col"),
        check_vma=False,
    )
```
